512 devices in a mesh: dp: 64 (over x, y, z_hi), tensor: 8 (over z_lo, core).
Axes of the slice: x: 4, y: 4, z: 16 (z_hi: 4, z_lo: 4; z = z_hi * 4 + z_lo), core: 2. Of those that a mesh axis runs over, the one named last changes fastest.
Arguments:
- master: float32 [3, 8, 1024, 2048], P(None, None, 'dp', 'tensor'), may hold values from -6 to 6
- moment_one: float32 [3, 8, 1024, 2048], P(None, None, 'dp', 'tensor'), may hold values from -4 to 4
- moment_two: float32 [3, 8, 1024, 2048], P(None, None, 'dp', 'tensor'), may hold values from 0.01 to 1
- gradients: bfloat16 [3, 8, 1024, 2048], P(None, None, 'dp', 'tensor'), may hold values from -10000 to 10000
- norm_gain: float32 [2048], replicated, may hold values from 0.1 to 1.9
- hidden_in: bfloat16 [4, 2048, 2048], P(None, ('dp', 'tensor')), may hold values from -6 to 6
- expert_ids: int32 [4, 2048, 2], P(None, ('dp', 'tensor')), may hold values from 0 to 7, all different within a row; in each aligned block of 4 rows (0 to 3, 4 to 7, ..., all dimensions but the last counted through in order) at most 2 rows name the same one
- route_weights: float32 [4, 2048, 2], P(None, ('dp', 'tensor')), may hold values from 0.05 to 1
Outputs:
- new_master: float32 [3, 8, 1024, 2048], P(None, None, 'dp', 'tensor')
- new_moment_one: float32 [3, 8, 1024, 2048], P(None, None, 'dp', 'tensor')
- new_moment_two: float32 [3, 8, 1024, 2048], P(None, None, 'dp', 'tensor')
- served_weights: bfloat16 [3, 8192, 2048], P(None, 'dp')
- decoded: bfloat16 [4, 2048, 2048], P(None, ('dp', 'tensor'))
The draws below stay inside these ranges and needn't reach their ends.
Inputs may be any that keep to these rules, and one draw needn't show every extreme that they name: `expert_ids`: A row names 2 different experts; in each step the 4 rows of one device name one expert at most 2 times.
All inputs are finite; a program needn't handle non-finite values.
Results may differ from the reference program's by a relative error of at most 0.0067.
Values may be sent and summed in bfloat16 or wider, within the bound.
A program may use at most 64 MiB of HBM per device.

```python
import math
import jax
import jax.numpy as jnp
import numpy as np
from jax import lax

D = 2048
FF = 1024
FF_DEV = 128
TOP = 2
STEPS = 4
ROWS_DEV = 4
GROUP = 8
EXPERTS = 8
STRIP = 2
CAP = 2
TOKENS = 2048
COUNT = 50331648
N_DP = 64


def draw_gradients(key, part):
    subkeys = jax.random.split(jax.random.fold_in(key, 7), 3)
    full_shape = (3, EXPERTS, FF, D)
    random_part = jnp.clip(jax.random.normal(subkeys[0], full_shape, jnp.float32), -5.0, 5.0)
    row_scale = jnp.exp(jax.random.uniform(subkeys[1], (3, EXPERTS, FF, 1), jnp.float32) * math.log(10.0))
    column_scale = jnp.exp(jax.random.uniform(subkeys[2], (D,), jnp.float32) * math.log(10.0))
    unit_ramp = jnp.exp(0.5 * math.log(3.0) * jnp.arange(FF, dtype=jnp.float32) / FF)
    width_ramp = jnp.exp(0.5 * math.log(3.0) * jnp.arange(D, dtype=jnp.float32) / D)
    values = random_part * row_scale * column_scale * unit_ramp[:, None] * width_ramp
    return values.astype(jnp.bfloat16)


def levels(key, extent, shards, smallest, top_value):
    def one(position, blocks):
        draws = jax.random.uniform(jax.random.fold_in(jax.random.fold_in(key, 6), position), (blocks,), jnp.float32, smallest / len(shards), top_value / len(shards))
        return jnp.repeat(jnp.exp(draws), extent[position] // blocks).reshape((-1,) + (1,) * (len(extent) - position - 1))

    level = one(*shards[0])
    for cut in shards[1:]:
        level = level * one(*cut)
    return level


def shared_out(rng, own, number, rows, count, top, bound, skew):
    ranking = jax.random.permutation(rng, count)
    crowded, usual = load_shares(count, rows * top, bound, skew, True), load_shares(count, rows * top, bound, skew, False)
    places = jnp.arange(count)

    def named(tallies, offset_by):
        used = int((tallies > 0).sum())
        fixed = max(1, used // 4)
        moved = fixed + (places - fixed + offset_by * (used - fixed)) % max(1, count - fixed)
        return jnp.zeros((count,), jnp.int32).at[ranking[jnp.where(places < fixed, places, moved)]].set(jnp.asarray(tallies, jnp.int32))

    tallies = jnp.where(number % 4 == 0, named(crowded, number // 4), named(usual, number - number // 4 - 1))
    mixed = jax.random.permutation(jax.random.fold_in(own, 3), count)
    donor, receiver = mixed[0:count // 2 * 2:2], mixed[1:count // 2 * 2:2]
    slack = jnp.minimum(tallies[donor] - 1, bound - tallies[receiver]) // 2
    slack = jnp.where((donor == ranking[0]) | (receiver == ranking[0]) | (tallies[receiver] == 0), 0, jnp.maximum(slack, 0))
    moved = jax.random.randint(jax.random.fold_in(own, 4), (count // 2,), 0, 1 << 20) % (slack + 1)
    tallies = tallies.at[donor].add(-moved).at[receiver].add(moved)
    members = jnp.searchsorted(jnp.cumsum(tallies), jnp.arange(rows * top), side="right").astype(jnp.int32)
    listing = members.reshape(top, rows).T
    listing = listing[jax.random.permutation(jax.random.fold_in(own, 1), rows)]
    offset_by = jax.random.randint(jax.random.fold_in(own, 2), (rows, 1), 0, top)
    return jnp.take_along_axis(listing, (jnp.arange(top)[None, :] + offset_by) % top, axis=1)


def load_shares(count, total, most, slope, full):
    weights = [(1 << 20) // math.isqrt(rank ** slope) + 1 for rank in range(1, count + 1)]
    largest = most if full else min(most, max(-(-total // count), total * weights[0] // sum(weights)))
    least = 1 if total - largest >= count - 1 else 0
    holding, rest = [largest] + [least] * (count - 1), total - largest - least * (count - 1)
    while rest > 0:
        movable = [i for i in range(1, count) if holding[i] < largest] or [i for i in range(1, count) if holding[i] < most]
        pool, left = sum([weights[i] for i in movable]), rest
        for i in movable:
            extra = min(most - holding[i], max(1, left * weights[i] // pool), rest)
            holding[i] = holding[i] + extra
            rest = rest - extra
    return np.array(holding)


def normal_values(own_key, shape, width, most, shards=(), kind=jnp.bfloat16):
    drawn = jax.random.normal(own_key, shape, jnp.float32) * width
    if len(shards) > 0:
        drawn = levels(own_key, shape, shards, -0.22, 0.18) * drawn
    return jnp.clip(drawn, min=-most, max=most).astype(kind)


def setup_inputs(seed: int = 0) -> dict:
    key_of = jax.random.split(jax.random.key(seed), 9)
    master = normal_values(key_of[0], (3, EXPERTS, FF, D), 1.0, 6.0, ((2, 64), (3, 8)), jnp.float32)
    moment_one = normal_values(key_of[1], (3, EXPERTS, FF, D), 0.3, 4.0, ((2, 64), (3, 8)), jnp.float32)
    moment_two = jnp.clip(jnp.exp(math.log(1.0) - 4.6051702 * jax.random.uniform(key_of[2], (3, EXPERTS, FF, D), jnp.float32) ** levels(key_of[2], (3, EXPERTS, FF, D), ((2, 64), (3, 8)), -0.2, 0.2)), 0.01, 1.0)
    gradients = draw_gradients(jax.random.fold_in(key_of[8], 71), 0)
    norm_gain = jnp.clip(1.0 + 0.18 * jax.random.normal(key_of[4], (D,), jnp.float32), 0.1, 1.9)
    hidden_in = normal_values(key_of[5], (STEPS, TOKENS, D), 1.0, 6.0, ((1, 512),))
    expert_ids_keys = jax.random.split(jax.random.fold_in(key_of[6], 1), STEPS * TOKENS // ROWS_DEV)
    expert_ids_turns = jax.random.permutation(jax.random.fold_in(key_of[6], 3), STEPS * TOKENS // ROWS_DEV)
    expert_ids = jax.vmap(lambda own, number: shared_out(jax.random.fold_in(key_of[6], 2), own, number, ROWS_DEV, EXPERTS, TOP, CAP, 1))(expert_ids_keys, expert_ids_turns).reshape((STEPS, TOKENS, TOP))
    route_weights = jnp.clip(jnp.exp(math.log(1.0) - 2.9957323 * jax.random.uniform(key_of[7], (STEPS, TOKENS, TOP), jnp.float32) ** levels(key_of[7], (STEPS, TOKENS, TOP), ((1, 512),), -0.2, 0.2)), 0.05, 1.0)
    return {"master": master, "moment_one": moment_one, "moment_two": moment_two, "gradients": gradients, "norm_gain": norm_gain, "hidden_in": hidden_in, "expert_ids": expert_ids, "route_weights": route_weights}


beta_one = 0.9
beta_two = 0.95
learn_rate = 0.02
decay_rate = 0.1
adam_eps = 1e-08
step_count = 10
norm_eps = 1e-06

def adam_update(master, moment_one, moment_two, gradients, clip_factor):
    scaled = gradients.astype(jnp.float32) * clip_factor
    first_moment = beta_one * moment_one + (1.0 - beta_one) * scaled
    second = beta_two * moment_two + (1.0 - beta_two) * scaled * scaled
    first_fix = 1.0 - beta_one ** step_count
    second_fix = 1.0 - beta_two ** step_count
    update = first_moment / first_fix / (jnp.sqrt(second / second_fix) + adam_eps)
    return (master - learn_rate * (update + decay_rate * master), first_moment, second)

def decode_step(token_rows, step_ids, step_gates, into_weights, down_weights, norm_gain):
    widened = token_rows.astype(jnp.float32)
    factor = lax.rsqrt(lax.optimization_barrier(jnp.mean(widened * widened, axis=1, keepdims=True)) + norm_eps)
    normed = (widened * factor * norm_gain).astype(jnp.bfloat16)
    shares = step_gates / lax.optimization_barrier(jnp.sum(step_gates, axis=1, keepdims=True))
    pair_keys = step_ids.reshape(-1).astype(jnp.int32)
    pair_order = jnp.argsort(pair_keys, stable=True).astype(jnp.int32)
    owner_row = pair_order // TOP
    picked = normed[owner_row]
    counts = lax.optimization_barrier(jnp.sum((pair_keys[:, None] == jnp.arange(EXPERTS, dtype=jnp.int32)[None, :]).astype(jnp.int32), axis=0)).astype(jnp.int32)
    projected = lax.ragged_dot(picked, into_weights, counts, preferred_element_type=jnp.float32) / math.sqrt(D)
    active = (jax.nn.silu(projected[:, :FF]) * projected[:, FF:]).astype(jnp.bfloat16)
    summed = jnp.zeros((pair_keys.shape[0], D), jnp.float32)
    for group_index in range(GROUP):
        lower = group_index * FF_DEV
        group_part = lax.ragged_dot(active[:, lower:lower + FF_DEV], down_weights[:, lower:lower + FF_DEV, :], counts, preferred_element_type=jnp.float32)
        rounded = (group_part / math.sqrt(FF)).astype(jnp.bfloat16)
        rounded = lax.optimization_barrier(rounded)
        summed = summed + rounded.astype(jnp.float32)
    weight = shares.reshape(-1)[pair_order]
    result = widened.at[owner_row].add(weight[:, None] * summed)
    return result.astype(jnp.bfloat16)

def reference(master, moment_one, moment_two, gradients, norm_gain, hidden_in, expert_ids, route_weights):
    widened = gradients.astype(jnp.float32)
    squares = jnp.sum(widened * widened)
    clip_factor = jnp.minimum(1.0, lax.rsqrt(squares / COUNT + norm_eps))
    new_master, new_one, new_two = adam_update(master, moment_one, moment_two, gradients, clip_factor)
    rounded = new_master.astype(jnp.bfloat16)
    regrouped = rounded.reshape(3, EXPERTS, N_DP, GROUP, STRIP, D)
    served = jnp.transpose(regrouped, (0, 1, 3, 2, 4, 5)).reshape(3, EXPERTS * FF, D)
    weights = served.reshape(3, EXPERTS, FF, D)
    into_weights = jnp.swapaxes(jnp.concatenate([weights[0], weights[1]], axis=1), 1, 2)
    decoded_steps = []
    for step_index in range(STEPS):
        decoded_steps.append(decode_step(hidden_in[step_index], expert_ids[step_index], route_weights[step_index], into_weights, weights[2], norm_gain))
    return (new_master, new_one, new_two, served, jnp.stack(decoded_steps))
```

```python
import math

import jax
import jax.numpy as jnp
from jax import lax
from jax.experimental import pallas as pl
from jax.experimental.pallas import tpu as pltpu
from jax.sharding import Mesh
from jax.sharding import PartitionSpec as P

DP = ("dp_0", "dp_1", "dp_2")
TENSOR = ("tensor_0", "tensor_1")
DP_TENSOR = DP + TENSOR
X_AXIS, Y_AXIS, ZH_AXIS, ZL_AXIS, C_AXIS = DP_TENSOR

MESH = pl.DeviceIdType.MESH
F32 = jnp.float32
BF16 = jnp.bfloat16

beta_one = 0.9
beta_two = 0.95
learn_rate = 0.02
decay_rate = 0.1
adam_eps = 1e-08
step_count = 10
norm_eps = 1e-06

WIDTH = 2048
PART = 256
HIDDEN = 1024
COUNT = 3 * 8 * 1024 * 2048
BLOCK = 32


def one_hot_rows(source_of):
    row = lax.broadcasted_iota(jnp.int32, (128, 128), 0)
    column = lax.broadcasted_iota(jnp.int32, (128, 128), 1)
    a, b, c, i = row // 32, (row // 8) % 4, (row // 2) % 4, row % 2
    return jnp.where(column == source_of(a, b, c, i), 1.0, 0.0).astype(BF16)


def matmul(left, right):
    return lax.dot_general(left, right, (((1,), (0,)), ((), ())), preferred_element_type=F32)


def matmul_nt(left, right):
    return lax.dot_general(left, right, (((1,), (1,)), ((), ())), preferred_element_type=F32)


def body(
    ids_ref,
    gates_ref,
    master_ref,
    one_ref,
    two_ref,
    grad_ref,
    gain_ref,
    hidden_ref,
    new_master_ref,
    new_one_ref,
    new_two_ref,
    served_ref,
    decoded_ref,
    wide,
    zrows,
    meta,
    sums_out,
    sums_in,
    stage,
    slots,
    answers,
    from_partner,
    relay,
    joined,
    back,
    parts,
    parts_in,
    wz_out,
    wz_in,
    wy_out,
    wy_in,
    wx_out,
    sum_sem,
    meta_sem,
    tok_sem,
    x_sem,
    y_sem,
    ret_sem,
    wz_sem,
    wy_sem,
    wx_sem,
    wl_sem,
    wc_sem,
):
    x = lax.axis_index(X_AXIS)
    y = lax.axis_index(Y_AXIS)
    zh = lax.axis_index(ZH_AXIS)
    zl = lax.axis_index(ZL_AXIS)
    core = lax.axis_index(C_AXIS)
    pair = y // 2
    odd = y % 2
    partner = y + 1 - 2 * odd
    other = (y + 3 + 2 * odd) % 4
    started = []

    def send(source, target, sems, index, device):
        copy = pltpu.make_async_remote_copy(
            src_ref=source,
            dst_ref=target,
            send_sem=sems.at[(0,) + index],
            recv_sem=sems.at[(1,) + index],
            device_id=device,
            device_id_type=MESH,
        )
        copy.start()
        started.append(copy)
        return copy

    def turn(axis, me, j):
        return {axis: (me + j) % 4}

    barrier = pltpu.get_barrier_semaphore()
    for axis, me in ((X_AXIS, x), (Y_AXIS, y), (ZH_AXIS, zh), (ZL_AXIS, zl)):
        for j in (1, 2, 3):
            pl.semaphore_signal(barrier, inc=1, device_id=turn(axis, me, j), device_id_type=MESH)
    pl.semaphore_signal(barrier, inc=1, device_id={C_AXIS: 1 - core}, device_id_type=MESH)

    for s in range(4):
        wide[pl.ds(4 * s, 4), :] = hidden_ref[s].astype(F32)
    rows = wide[...]
    factor = lax.rsqrt(jnp.mean(rows * rows, axis=1, keepdims=True) + norm_eps)
    zrows[zh] = (rows * factor * gain_ref[...]).astype(BF16)
    meta_row = lax.broadcasted_iota(jnp.int32, (8, 128), 0)
    meta_lane = lax.broadcasted_iota(jnp.int32, (8, 128), 1) - zh * 16
    tile = jnp.zeros((8, 128), F32)
    for s in range(4):
        for r in range(4):
            for k in range(2):
                spot = meta_lane == 4 * s + r
                tile = jnp.where(spot & (meta_row == k), ids_ref[s, r, k].astype(F32), tile)
                tile = jnp.where(spot & (meta_row == 2 + k), gates_ref[s, r, k], tile)
    meta[0] = tile
    squares = jnp.zeros((8, 128), F32)
    for block in range(12):
        values = grad_ref[pl.ds(32 * block, 32), :].astype(F32)
        values = values * values
        for i in range(4):
            for h in range(2):
                squares = squares + values[8 * i : 8 * i + 8, 128 * h : 128 * h + 128]
    sums_out[0] = squares
    pl.semaphore_wait(barrier, 13)

    phases = ((ZL_AXIS, zl), (ZH_AXIS, zh), (X_AXIS, x), (Y_AXIS, y))
    token_copies = []
    for phase, (axis, me) in enumerate(phases):
        copies = [
            send(
                sums_out.at[phase],
                sums_in.at[phase, j - 1],
                sum_sem,
                (phase, j - 1),
                turn(axis, me, j),
            )
            for j in (1, 2, 3)
        ]
        if phase == 1:
            for j in (1, 3, 2):
                token_copies.append(
                    send(meta.at[0], meta.at[j], meta_sem, (j - 1,), turn(ZH_AXIS, zh, j))
                )
                token_copies.append(
                    send(zrows.at[zh], zrows.at[zh], tok_sem, (j - 1,), turn(ZH_AXIS, zh, j))
                )
        for copy in copies:
            copy.wait_recv()
        squares = squares + sums_in[phase, 0] + sums_in[phase, 1] + sums_in[phase, 2]
        sums_out[phase + 1] = squares
    copy = send(sums_out.at[4], sums_in.at[4, 0], sum_sem, (4, 0), {C_AXIS: 1 - core})
    permute_z = one_hot_rows(lambda a, b, c, i: ((b * 4 + c) * 4 + a) * 2 + i)
    permute_y = one_hot_rows(lambda a, b, c, i: ((c * 4 + b) * 4 + a) * 2 + i)
    permute_x = one_hot_rows(lambda a, b, c, i: ((b * 4 + a) * 4 + c) * 2 + i)
    copy.wait_recv()
    squares = squares + sums_in[4, 0]
    total = jnp.sum(squares, axis=(0, 1), keepdims=True)
    clip = jnp.minimum(1.0, lax.rsqrt(total * (1.0 / COUNT) + norm_eps))

    first_fix = 1.0 / (1.0 - beta_one**step_count)
    second_fix = 1.0 / (1.0 - beta_two**step_count)
    z_copies = []
    for k in range(3):
        for half in range(4):
            at = pl.ds(128 * k + 32 * half, 32)
            scaled = grad_ref[at, :].astype(F32) * clip
            first = beta_one * one_ref[at, :] + (1.0 - beta_one) * scaled
            second = beta_two * two_ref[at, :] + (1.0 - beta_two) * scaled * scaled
            update = first * first_fix / (jnp.sqrt(second * second_fix) + adam_eps)
            old = master_ref[at, :]
            new_master_ref[at, :] = old - learn_rate * (update + decay_rate * old)
            new_one_ref[at, :] = first
            new_two_ref[at, :] = second
        rounded = new_master_ref[pl.ds(128 * k, 128), :].astype(BF16)
        wz_out[k] = matmul(permute_z, rounded).astype(BF16).reshape(4, 32, PART)
        for j in (2, 1, 3):
            z_copies.append(
                send(
                    wz_out.at[k, (zh + j) % 4],
                    wz_in.at[k, zh],
                    wz_sem,
                    (k, j - 1),
                    turn(ZH_AXIS, zh, j),
                )
            )
        wz_in[k, zh] = wz_out[k, zh]

    for copy in token_copies:
        copy.wait_recv()
    routes = meta[0] + meta[1] + meta[2] + meta[3]
    id_one, id_two = routes[0:1, 0:64], routes[1:2, 0:64]
    gate_one, gate_two = routes[2:3, 0:64], routes[3:4, 0:64]
    gate_sum = gate_one + gate_two
    share_one, share_two = gate_one / gate_sum, gate_two / gate_sum
    place = lax.broadcasted_iota(jnp.int32, (8, 64), 0)
    expert = (2 * ((x + place // 2) % 4) + (pair + place % 2) % 2).astype(F32)
    names_one = jnp.where(id_one == expert, 1.0, 0.0)
    names_two = jnp.where(id_two == expert, 1.0, 0.0)
    named = names_one + names_two
    share = names_one * share_one + names_two * share_two
    above = lax.broadcasted_iota(jnp.int32, (64, 64), 0)
    below = lax.broadcasted_iota(jnp.int32, (64, 64), 1)
    before = jnp.where((above // 4 == below // 4) & (above < below), 1.0, 0.0).astype(BF16)
    earlier = matmul(named.astype(BF16), before)
    slot_row = lax.broadcasted_iota(jnp.int32, (32, 64), 0)
    row_lane = lax.broadcasted_iota(jnp.int32, (32, 64), 1)
    same_block = jnp.where(slot_row // 2 == row_lane // 4, 1.0, 0.0)
    slot_number = (slot_row % 2).astype(F32)
    token_rows = zrows[...].reshape(64, WIDTH)
    weights = []
    x_copies = {}
    for d in (0, 2, 1, 3):
        picks = []
        for r in range(2):
            p = 2 * d + r
            hit = jnp.where(earlier[p : p + 1, :] == slot_number, same_block, 0.0)
            picks.append(hit * named[p : p + 1, :])
        chosen = matmul(jnp.concatenate(picks, axis=0).astype(BF16), token_rows)
        chosen = chosen.astype(BF16).reshape(2, BLOCK, WIDTH)
        if d == 0:
            slots[0, 0] = chosen[0]
            slots[1, 0] = chosen[1]
        else:
            stage[d - 1] = chosen
            x_copies[d] = send(
                stage.at[d - 1], slots.at[pl.ds(0, 2), d], x_sem, (0, d), turn(X_AXIS, x, d)
            )
    for p in range(8):
        hit = jnp.where(earlier[p : p + 1, :] == slot_number, same_block, 0.0)
        weights.append(hit * share[p : p + 1, :])

    y_copies = []
    for k in range(3):
        for copy in z_copies[3 * k : 3 * k + 3]:
            copy.wait_recv()
        gathered = wz_in[k].reshape(128, PART)
        wy_out[k] = matmul(permute_y, gathered).astype(BF16).reshape(4, 32, PART)
        for j in (2, 1, 3):
            y_copies.append(
                send(
                    wy_out.at[k, (y + j) % 4],
                    wy_in.at[k, y],
                    wy_sem,
                    (k, j - 1),
                    turn(Y_AXIS, y, j),
                )
            )
        wy_in[k, y] = wy_out[k, y]

    to_partner, to_other, onward = {}, {}, {}
    order = (0, 1, 3, 2)

    def spread(d):
        if d:
            x_copies[d].wait_recv()
        to_other[d] = send(
            slots.at[1, d], slots.at[3, d], y_sem, (1, d), {Y_AXIS: other}
        )
        to_partner[d] = send(
            slots.at[0, d], slots.at[2, d], y_sem, (0, d), {Y_AXIS: partner}
        )

    def forward(d):
        to_other[d].wait_recv()
        onward[d] = send(slots.at[3, d], slots.at[4, d], y_sem, (2, d), {Y_AXIS: partner})

    spread(0)
    t = (2 * zl + core) * PART
    columns = pl.ds(pl.multiple_of(t, PART), PART)
    own_rows = pl.ds(pl.multiple_of(32 * x, 32), 32)
    wx_copies = []
    for k in range(3):
        for copy in y_copies[3 * k : 3 * k + 3]:
            copy.wait_recv()
        gathered = wy_in[k].reshape(128, PART)
        wx_out[k] = matmul(permute_x, gathered).astype(BF16).reshape(4, 32, PART)
        for j in (2, 1, 3):
            wx_copies.append(
                send(
                    wx_out.at[k, (x + j) % 4],
                    served_ref.at[k, own_rows, columns],
                    wx_sem,
                    (k, j - 1),
                    turn(X_AXIS, x, j),
                )
            )
        served_ref[k, own_rows, columns] = wx_out[k, x]

    line_copies = []
    core_copies = []
    for k in range(3):
        for copy in wx_copies[3 * k : 3 * k + 3]:
            copy.wait_recv()
        mine = served_ref.at[k, :, columns]
        for j in (1, 3, 2):
            line_copies.append((k, j, send(mine, mine, wl_sem, (k, j - 1), turn(ZL_AXIS, zl, j))))
        core_copies.append(send(mine, mine, wc_sem, (k, 0), {C_AXIS: 1 - core}))
    spread(1)
    forward(0)
    spread(3)
    forward(1)
    spread(2)
    forward(3)
    for k, j, copy in line_copies:
        copy.wait_recv()
        theirs = (2 * ((zl + 4 - j) % 4) + core) * PART
        piece = served_ref.at[k, :, pl.ds(pl.multiple_of(theirs, PART), PART)]
        core_copies.append(send(piece, piece, wc_sem, (k, j), {C_AXIS: 1 - core}))
    forward(2)
    for copy in core_copies:
        copy.wait_recv()
    for d in order:
        to_partner[d].wait_recv()
        onward[d].wait_recv()

    for number, origin in ((3, 4), (1, 2), (2, 3), (0, 0)):
        taken = slots[origin].reshape(4 * BLOCK, WIDTH)
        gate = matmul_nt(taken, served_ref[0]) * (1.0 / math.sqrt(WIDTH))
        up = matmul_nt(taken, served_ref[1]) * (1.0 / math.sqrt(WIDTH))
        active = (gate / (1.0 + jnp.exp(-gate)) * up).astype(BF16)
        for h in range(4):
            span = pl.ds(512 * h, 512)
            out = matmul(active, served_ref[2, :, span]) * (1.0 / math.sqrt(HIDDEN))
            answers[number, :, :, span] = out.astype(BF16).reshape(4, BLOCK, 512)
        if number == 3 or number == 1:
            for d in (2, 1, 3, 0):
                started_copy = send(
                    answers.at[number, d],
                    from_partner.at[number // 2, d],
                    ret_sem,
                    (number // 2, d),
                    {Y_AXIS: partner},
                )
                if number == 3:
                    to_other[d] = started_copy
                else:
                    to_partner[d] = started_copy

    for d in (2, 1, 3, 0):
        to_other[d].wait_recv()
        both = answers[2, d].astype(F32) + from_partner[1, d].astype(F32)
        relay[d] = both.astype(BF16)
        onward[d] = send(relay.at[d], joined.at[1, d], ret_sem, (2, d), {Y_AXIS: other})
    for d in (2, 1, 3, 0):
        to_partner[d].wait_recv()
        both = answers[0, d].astype(F32) + from_partner[0, d].astype(F32)
        joined[0, d] = both.astype(BF16)
        onward[d].wait_recv()
        if d:
            x_copies[d] = send(
                joined.at[pl.ds(0, 2), d], back.at[d - 1], x_sem, (1, d), turn(X_AXIS, x, 4 - d)
            )

    parted = []
    for d in range(4):
        weight = jnp.concatenate(weights[2 * d : 2 * d + 2], axis=0).T
        high = weight.astype(BF16)
        rest = weight - high.astype(F32)
        middle = rest.astype(BF16)
        low = (rest - middle.astype(F32)).astype(BF16)
        parted.append((high, middle, low))
    gathered_rows = jnp.zeros((64, WIDTH), F32)
    for d in (0, 1, 3, 2):
        if d:
            x_copies[d].wait_recv()
            held = back[d - 1].reshape(2 * BLOCK, WIDTH)
        else:
            held = joined[:, 0].reshape(2 * BLOCK, WIDTH)
        for piece in parted[d]:
            gathered_rows = gathered_rows + matmul(piece, held)
    parts[...] = gathered_rows.astype(BF16).reshape(4, 16, WIDTH)
    z_back = [
        send(parts.at[(zh + j) % 4], parts_in.at[j - 1], ret_sem, (3, j - 1), turn(ZH_AXIS, zh, j))
        for j in (2, 1, 3)
    ]
    result = wide[...] + parts[zh].astype(F32)
    for copy in z_back:
        copy.wait_recv()
    for j in range(3):
        result = result + parts_in[j].astype(F32)
    wide[...] = result
    for s in range(4):
        decoded_ref[s] = wide[pl.ds(4 * s, 4), :].astype(BF16)
    for copy in started:
        copy.wait_send()


def per_device(
    master, moment_one, moment_two, gradients, norm_gain, hidden_in, expert_ids, route_weights
):
    vmem = pl.BlockSpec(memory_space=pltpu.VMEM)
    smem = pl.BlockSpec(memory_space=pltpu.SMEM)
    flat = (384, PART)
    dma = pltpu.SemaphoreType.DMA
    new_master, new_one, new_two, served, decoded = pl.pallas_call(
        body,
        out_shape=(
            jax.ShapeDtypeStruct(flat, F32),
            jax.ShapeDtypeStruct(flat, F32),
            jax.ShapeDtypeStruct(flat, F32),
            jax.ShapeDtypeStruct((3, 128, WIDTH), BF16),
            jax.ShapeDtypeStruct((4, 4, WIDTH), BF16),
        ),
        in_specs=[smem, smem] + [vmem] * 6,
        out_specs=(vmem,) * 5,
        scratch_shapes=[
            pltpu.VMEM((16, WIDTH), F32),
            pltpu.VMEM((4, 16, WIDTH), BF16),
            pltpu.VMEM((4, 8, 128), F32),
            pltpu.VMEM((5, 8, 128), F32),
            pltpu.VMEM((5, 3, 8, 128), F32),
            pltpu.VMEM((3, 2, BLOCK, WIDTH), BF16),
            pltpu.VMEM((5, 4, BLOCK, WIDTH), BF16),
            pltpu.VMEM((4, 4, BLOCK, WIDTH), BF16),
            pltpu.VMEM((2, 4, BLOCK, WIDTH), BF16),
            pltpu.VMEM((4, BLOCK, WIDTH), BF16),
            pltpu.VMEM((2, 4, BLOCK, WIDTH), BF16),
            pltpu.VMEM((3, 2, BLOCK, WIDTH), BF16),
            pltpu.VMEM((4, 16, WIDTH), BF16),
            pltpu.VMEM((3, 16, WIDTH), BF16),
            pltpu.VMEM((3, 4, 32, PART), BF16),
            pltpu.VMEM((3, 4, 32, PART), BF16),
            pltpu.VMEM((3, 4, 32, PART), BF16),
            pltpu.VMEM((3, 4, 32, PART), BF16),
            pltpu.VMEM((3, 4, 32, PART), BF16),
            dma((2, 5, 3)),
            dma((2, 3)),
            dma((2, 3)),
            dma((2, 2, 4)),
            dma((2, 3, 4)),
            dma((2, 4, 4)),
            dma((2, 3, 3)),
            dma((2, 3, 3)),
            dma((2, 3, 3)),
            dma((2, 3, 3)),
            dma((2, 3, 4)),
        ],
        compiler_params=pltpu.CompilerParams(
            collective_id=0, has_side_effects=True, vmem_limit_bytes=48 * 1024 * 1024
        ),
        name="step",
    )(
        expert_ids,
        route_weights,
        master.reshape(flat),
        moment_one.reshape(flat),
        moment_two.reshape(flat),
        gradients.reshape(flat),
        norm_gain.reshape(1, WIDTH),
        hidden_in,
    )
    return (
        new_master.reshape(master.shape),
        new_one.reshape(master.shape),
        new_two.reshape(master.shape),
        served,
        decoded,
    )


def solution(mesh):
    split = Mesh(mesh.devices.reshape(4, 4, 4, 4, 2), DP_TENSOR)
    sharded = P(None, None, DP, TENSOR)
    by_row = P(None, DP_TENSOR, None)
    return jax.shard_map(
        per_device,
        mesh=split,
        in_specs=(sharded, sharded, sharded, sharded, P(), by_row, by_row, by_row),
        out_specs=(sharded, sharded, sharded, P(None, DP, None), by_row),
        check_vma=False,
    )
```

```python
import math

import jax
import jax.numpy as jnp
from jax import lax
from jax.experimental import pallas as pl
from jax.experimental.pallas import tpu as pltpu
from jax.sharding import Mesh
from jax.sharding import PartitionSpec as P

DP = ("dp_0", "dp_1", "dp_2")
TENSOR = ("tensor_0", "tensor_1")
DP_TENSOR = DP + TENSOR
X_AXIS, Y_AXIS, ZH_AXIS, ZL_AXIS, C_AXIS = DP_TENSOR

MESH = pl.DeviceIdType.MESH
F32 = jnp.float32
BF16 = jnp.bfloat16

beta_one = 0.9
beta_two = 0.95
learn_rate = 0.02
decay_rate = 0.1
adam_eps = 1e-08
step_count = 10
norm_eps = 1e-06

WIDTH = 2048
PART = 256
HIDDEN = 1024
COUNT = 3 * 8 * 1024 * 2048
BLOCK = 32


def one_hot_rows(source_of):
    row = lax.broadcasted_iota(jnp.int32, (128, 128), 0)
    column = lax.broadcasted_iota(jnp.int32, (128, 128), 1)
    a, b, c, i = row // 32, (row // 8) % 4, (row // 2) % 4, row % 2
    return jnp.where(column == source_of(a, b, c, i), 1.0, 0.0).astype(BF16)


def matmul(left, right):
    return lax.dot_general(left, right, (((1,), (0,)), ((), ())), preferred_element_type=F32)


def matmul_nt(left, right):
    return lax.dot_general(left, right, (((1,), (1,)), ((), ())), preferred_element_type=F32)


def body(
    ids_ref,
    gates_ref,
    master_hbm,
    one_hbm,
    two_hbm,
    grad_hbm,
    gain_hbm,
    hidden_hbm,
    new_master_hbm,
    new_one_hbm,
    new_two_hbm,
    served_hbm,
    decoded_hbm,
    new_master_ref,
    new_one_ref,
    new_two_ref,
    decoded_ref,
    master_ref,
    one_ref,
    two_ref,
    grad_ref,
    gain_ref,
    hidden_ref,
    wide,
    zrows,
    meta,
    sums_out,
    sums_in,
    stage,
    slots,
    answers,
    from_core,
    relay,
    joined,
    back,
    parts,
    parts_in,
    wz_out,
    wz_in,
    wy_out,
    wy_in,
    wx_out,
    wall,
    in_sem,
    out_sem,
    sum_sem,
    meta_sem,
    tok_sem,
    x_sem,
    y_sem,
    core_sem,
    ret_sem,
    back_sem,
    end_sem,
    wz_sem,
    wy_sem,
    wx_sem,
    wl_sem,
    wc_sem,
    wp_sem,
):
    x = lax.axis_index(X_AXIS)
    y = lax.axis_index(Y_AXIS)
    zh = lax.axis_index(ZH_AXIS)
    zl = lax.axis_index(ZL_AXIS)
    core = lax.axis_index(C_AXIS)
    pair = y // 2
    odd = y % 2
    partner = y + 1 - 2 * odd
    other = (y + 3 + 2 * odd) % 4
    next_core = {C_AXIS: 1 - core}
    started = []

    def send(source, target, sems, index, device):
        copy = pltpu.make_async_remote_copy(
            src_ref=source,
            dst_ref=target,
            send_sem=sems.at[(0,) + index],
            recv_sem=sems.at[(1,) + index],
            device_id=device,
            device_id_type=MESH,
        )
        copy.start()
        started.append(copy)
        return copy

    def turn(axis, me, j):
        return {axis: (me + j) % 4}

    def along_z(j):
        z = (4 * zh + zl + j) % 16
        return {ZH_AXIS: z // 4, ZL_AXIS: z % 4}

    barrier = pltpu.get_barrier_semaphore()
    peers = [along_z(j) for j in (8, 7, 9, 6, 10, 5, 11, 4, 12, 3, 13, 2, 14, 1, 15)]
    peers += [turn(axis, me, j) for axis, me in ((X_AXIS, x), (Y_AXIS, y)) for j in (2, 1, 3)]
    peers += [{Y_AXIS: partner, C_AXIS: 1 - core}, next_core]
    for peer in peers:
        pl.semaphore_signal(barrier, inc=1, device_id=peer, device_id_type=MESH)
    loads = [
        pltpu.make_async_copy(source, target, in_sem.at[number])
        for number, (source, target) in enumerate(
            (
                (hidden_hbm, hidden_ref),
                (gain_hbm, gain_ref),
                (grad_hbm, grad_ref),
                (master_hbm, master_ref),
                (one_hbm, one_ref),
                (two_hbm, two_ref),
            )
        )
    ]
    for load in loads:
        load.start()

    meta_row = lax.broadcasted_iota(jnp.int32, (8, 128), 0)
    meta_lane = lax.broadcasted_iota(jnp.int32, (8, 128), 1) - zh * 8
    tile = jnp.zeros((8, 128), F32)
    for s in range(4):
        for r in range(4):
            spot = meta_lane == 32 * (s // 2) + 4 * (s % 2) + r
            for k in range(2):
                tile = jnp.where(spot & (meta_row == k), ids_ref[s, k, r].astype(F32), tile)
                tile = jnp.where(spot & (meta_row == 2 + k), gates_ref[s, k, r], tile)
    meta[0] = tile
    loads[0].wait()
    loads[1].wait()
    for s in range(4):
        wide[pl.ds(4 * s, 4), :] = hidden_ref[s].astype(F32)
    rows = wide[...]
    factor = lax.rsqrt(jnp.mean(rows * rows, axis=1, keepdims=True) + norm_eps)
    normed = rows * factor * gain_ref[...]
    zrows[0, zh] = normed[0:8].astype(BF16)
    zrows[1, zh] = normed[8:16].astype(BF16)
    loads[2].wait()
    squares = jnp.zeros((8, 128), F32)
    for block in range(12):
        values = grad_ref[pl.ds(32 * block, 32), :].astype(F32)
        values = values * values
        for i in range(4):
            for h in range(2):
                squares = squares + values[8 * i : 8 * i + 8, 128 * h : 128 * h + 128]
    sums_out[0] = squares
    pl.semaphore_wait(barrier, len(peers))

    slot = 0
    token_copies = []
    for phase, devices in enumerate(
        (
            [along_z(j) for j in (8, 7, 9, 6, 10, 5, 11, 4, 12, 3, 13, 2, 14, 1, 15)],
            [turn(X_AXIS, x, j) for j in (2, 1, 3)],
            [turn(Y_AXIS, y, j) for j in (2, 1, 3)],
            [next_core],
        )
    ):
        copies = [
            send(sums_out.at[phase], sums_in.at[slot + i], sum_sem, (slot + i,), device)
            for i, device in enumerate(devices)
        ]
        if phase == 0:
            for j in (2, 1, 3):
                token_copies.append(
                    send(meta.at[0], meta.at[j], meta_sem, (j - 1,), turn(ZH_AXIS, zh, j))
                )
                token_copies.append(
                    send(zrows.at[:, zh], zrows.at[:, zh], tok_sem, (j - 1,), turn(ZH_AXIS, zh, j))
                )
        if phase == 3:
            permute_z = one_hot_rows(lambda a, b, c, i: ((b * 4 + c) * 4 + a) * 2 + i)
            permute_y = one_hot_rows(lambda a, b, c, i: ((c * 4 + b) * 4 + a) * 2 + i)
            permute_x = one_hot_rows(lambda a, b, c, i: ((b * 4 + a) * 4 + c) * 2 + i)
            for load in loads[3:]:
                load.wait()
        for i, copy in enumerate(copies):
            copy.wait_recv()
            squares = squares + sums_in[slot + i]
        slot += len(copies)
        if phase < 3:
            sums_out[phase + 1] = squares
    total = jnp.sum(squares, axis=(0, 1), keepdims=True)
    clip = jnp.minimum(1.0, lax.rsqrt(total * (1.0 / COUNT) + norm_eps))

    first_fix = 1.0 / (1.0 - beta_one**step_count)
    second_fix = 1.0 / (1.0 - beta_two**step_count)
    z_copies = []
    stores = []

    def keep(source, target):
        copy = pltpu.make_async_copy(source, target, out_sem.at[len(stores)])
        copy.start()
        stores.append(copy)

    for k in range(3):
        for block in range(4):
            at = pl.ds(128 * k + 32 * block, 32)
            scaled = grad_ref[at, :].astype(F32) * clip
            first = beta_one * one_ref[at, :] + (1.0 - beta_one) * scaled
            second = beta_two * two_ref[at, :] + (1.0 - beta_two) * scaled * scaled
            update = first * first_fix / (jnp.sqrt(second * second_fix) + adam_eps)
            old = master_ref[at, :]
            new_master_ref[at, :] = old - learn_rate * (update + decay_rate * old)
            new_one_ref[at, :] = first
            new_two_ref[at, :] = second
        rounded = new_master_ref[pl.ds(128 * k, 128), :].astype(BF16)
        wz_out[k] = matmul(permute_z, rounded).astype(BF16).reshape(4, 32, PART)
        for j in (2, 1, 3):
            z_copies.append(
                send(
                    wz_out.at[k, (zh + j) % 4],
                    wz_in.at[k, zh],
                    wz_sem,
                    (k, j - 1),
                    turn(ZH_AXIS, zh, j),
                )
            )
        wz_in[k, zh] = wz_out[k, zh]
    keep(new_master_ref, new_master_hbm)
    keep(new_one_ref, new_one_hbm)
    keep(new_two_ref, new_two_hbm)

    for copy in token_copies:
        copy.wait_recv()
    routes = meta[0] + meta[1] + meta[2] + meta[3]
    id_one, id_two = routes[0:1, 0:64], routes[1:2, 0:64]
    gate_one, gate_two = routes[2:3, 0:64], routes[3:4, 0:64]
    gate_sum = gate_one + gate_two
    share_one, share_two = gate_one / gate_sum, gate_two / gate_sum
    place = lax.broadcasted_iota(jnp.int32, (8, 64), 0)
    expert = (2 * ((x + place // 2) % 4) + (pair + place % 2) % 2).astype(F32)
    names_one = jnp.where(id_one == expert, 1.0, 0.0)
    names_two = jnp.where(id_two == expert, 1.0, 0.0)
    named = names_one + names_two
    share = names_one * share_one + names_two * share_two
    above = lax.broadcasted_iota(jnp.int32, (64, 64), 0)
    below = lax.broadcasted_iota(jnp.int32, (64, 64), 1)
    before = jnp.where((above // 4 == below // 4) & (above < below), 1.0, 0.0).astype(BF16)
    earlier = matmul(named.astype(BF16), before)
    slot_row = lax.broadcasted_iota(jnp.int32, (32, 64), 0)
    row_lane = lax.broadcasted_iota(jnp.int32, (32, 64), 1)
    same_block = jnp.where(slot_row // 2 == row_lane // 4, 1.0, 0.0)
    slot_number = (slot_row % 2).astype(F32)
    hits = [jnp.where(earlier[p : p + 1, :] == slot_number, same_block, 0.0) for p in range(8)]
    token_rows = zrows[...].reshape(64, WIDTH)
    x_copies = {}
    for d in (0, 2, 1, 3):
        picks = [hits[2 * d + r] * named[2 * d + r : 2 * d + r + 1, :] for r in (1, 0)]
        chosen = matmul(jnp.concatenate(picks, axis=0).astype(BF16), token_rows)
        chosen = chosen.astype(BF16).reshape(2, BLOCK, WIDTH)
        if d == 0:
            slots[0, 0] = chosen[0]
            slots[1, 0] = chosen[1]
        else:
            stage[d - 1] = chosen
            x_copies[d] = send(
                stage.at[d - 1], slots.at[pl.ds(0, 2), d], x_sem, (d - 1,), turn(X_AXIS, x, d)
            )
    weights = []
    for h in range(2):
        columns = [hits[p] * share[p : p + 1, :] for p in range(8)]
        columns = [c[16 * h : 16 * h + 16, 32 * h : 32 * h + 32] for c in columns]
        weight = jnp.concatenate(columns, axis=0).T
        high = weight.astype(BF16)
        rest = weight - high.astype(F32)
        middle = rest.astype(BF16)
        low = (rest - middle.astype(F32)).astype(BF16)
        weights.append((high, middle, low))

    y_copies = []
    for k in range(3):
        for copy in z_copies[3 * k : 3 * k + 3]:
            copy.wait_recv()
        gathered = wz_in[k].reshape(128, PART)
        wy_out[k] = matmul(permute_y, gathered).astype(BF16).reshape(4, 32, PART)
        for j in (2, 1, 3):
            y_copies.append(
                send(
                    wy_out.at[k, (y + j) % 4],
                    wy_in.at[k, y],
                    wy_sem,
                    (k, j - 1),
                    turn(Y_AXIS, y, j),
                )
            )
        wy_in[k, y] = wy_out[k, y]

    over_y, over_core = {}, []

    def spread(d):
        if d:
            x_copies[d].wait_recv()
        over_y[d] = send(slots.at[0, d], slots.at[3, d], y_sem, (d,), {Y_AXIS: other})
        over_core.append(send(slots.at[1, d], slots.at[2, d], core_sem, (0, d), next_core))

    def forward(d):
        over_y[d].wait_recv()
        over_core.append(send(slots.at[3, d], slots.at[4, d], core_sem, (1, d), next_core))

    spread(0)

    def columns_of(position):
        return pl.ds(pl.multiple_of((2 * position + core) * PART, PART), PART)

    own_rows = pl.ds(pl.multiple_of(32 * x, 32), 32)
    wx_copies = []
    for k in range(3):
        for copy in y_copies[3 * k : 3 * k + 3]:
            copy.wait_recv()
        gathered = wy_in[k].reshape(128, PART)
        wx_out[k] = matmul(permute_x, gathered).astype(BF16).reshape(4, 32, PART)
        for j in (2, 1, 3):
            wx_copies.append(
                send(
                    wx_out.at[k, (x + j) % 4],
                    wall.at[odd, k, own_rows, columns_of(zl)],
                    wx_sem,
                    (k, j - 1),
                    turn(X_AXIS, x, j),
                )
            )
        wall[odd, k, own_rows, columns_of(zl)] = wx_out[k, x]

    across = {Y_AXIS: partner, C_AXIS: odd}
    line_copies = []
    core_copies = []

    def share_out(k, j, position):
        piece = wall.at[odd, k, :, columns_of(position)]
        send(piece, piece, wp_sem, (k, 2 * j + core), across)
        core_copies.append(send(piece, piece, wc_sem, (k, j), next_core))

    for k in range(3):
        for copy in wx_copies[3 * k : 3 * k + 3]:
            copy.wait_recv()
        mine = wall.at[odd, k, :, columns_of(zl)]
        for j in (2, 1, 3):
            line_copies.append((k, j, send(mine, mine, wl_sem, (k, j - 1), turn(ZL_AXIS, zl, j))))
        share_out(k, 0, zl)
    spread(1)
    forward(0)
    spread(3)
    forward(1)
    spread(2)
    for k, j, copy in line_copies:
        copy.wait_recv()
        share_out(k, j, (zl + 4 - j) % 4)
    forward(3)
    forward(2)
    for copy in core_copies:
        copy.wait_recv()
    keep(wall.at[odd], served_hbm)
    for copy in over_core:
        copy.wait_recv()

    @pl.when(core != odd)
    def _():
        for k in range(3):
            for number in range(8):
                piece = wall.at[core, k, :, pl.ds(PART * number, PART)]
                pltpu.make_async_remote_copy(
                    src_ref=piece,
                    dst_ref=piece,
                    send_sem=wp_sem.at[0, k, number],
                    recv_sem=wp_sem.at[1, k, number],
                    device_id=across,
                    device_id_type=MESH,
                ).wait_recv()

    into = wall.at[core, pl.ds(0, 2)]
    swaps = []
    for h in range(2):
        taken = slots[pl.ds(1, 4), :, pl.ds(16 * h, 16), :].reshape(256, WIDTH)
        projected = matmul_nt(taken, into[...].reshape(256, WIDTH)) * (1.0 / math.sqrt(WIDTH))
        gate, up = projected[:, :128], projected[:, 128:]
        active = (gate / (1.0 + jnp.exp(-gate)) * up).astype(BF16)
        for i in range(4):
            span = pl.ds(512 * i, 512)
            out = matmul(active, wall[core, 2, :, span]) * (1.0 / math.sqrt(HIDDEN))
            answers[h, :, :, :, span] = out.astype(BF16).reshape(4, 4, 16, 512)
        for number in (3, 1):
            swaps.append(
                send(
                    answers.at[h, number],
                    from_core.at[h, number // 2],
                    ret_sem,
                    (h, number // 2),
                    next_core,
                )
            )

    over_y = []
    for h in range(2):
        swaps[2 * h].wait_recv()
        relay[h] = (answers[h, 2].astype(F32) + from_core[h, 1].astype(F32)).astype(BF16)
        over_y.append(send(relay.at[h], joined.at[h, 1], ret_sem, (h, 2), {Y_AXIS: other}))
        swaps[2 * h + 1].wait_recv()
        joined[h, 0] = (answers[h, 0].astype(F32) + from_core[h, 0].astype(F32)).astype(BF16)
    over_x = []
    for h in range(2):
        over_y[h].wait_recv()
        for d in (2, 1, 3):
            over_x.append(
                send(joined.at[h, :, d], back.at[h, d], back_sem, (h, d), turn(X_AXIS, x, 4 - d))
            )
        back[h, 0] = joined[h, :, 0]

    over_z = []
    for h in range(2):
        for copy in over_x[3 * h : 3 * h + 3]:
            copy.wait_recv()
        held = back[h].reshape(128, WIDTH)
        made = matmul(weights[h][0], held) + matmul(weights[h][1], held) + matmul(weights[h][2], held)
        made = made.reshape(4, 8, WIDTH)
        parts[h] = made.astype(BF16)
        for j in (2, 1, 3):
            over_z.append(
                send(
                    parts.at[h, (zh + j) % 4],
                    parts_in.at[h, j - 1],
                    end_sem,
                    (h, j - 1),
                    turn(ZH_AXIS, zh, j),
                )
            )
    for h in range(2):
        result = wide[pl.ds(8 * h, 8), :] + parts[h, zh].astype(F32)
        for copy in over_z[3 * h : 3 * h + 3]:
            copy.wait_recv()
        for j in range(3):
            result = result + parts_in[h, j].astype(F32)
        decoded_ref[2 * h] = result[0:4].astype(BF16)
        decoded_ref[2 * h + 1] = result[4:8].astype(BF16)
    keep(decoded_ref, decoded_hbm)
    for copy in stores:
        copy.wait()
    for copy in started:
        copy.wait_send()


def hand_out(*refs):
    sources, targets, held, in_sem, out_sem = refs[:5], refs[5:10], refs[10:15], refs[15], refs[16]
    pieces = [(i, ()) for i in (0, 1, 2)] + [(3, (k,)) for k in range(3)] + [(4, ())]

    def piece(refs, i, at):
        return refs[i].at[at] if at else refs[i]

    loads, stores = [], []
    for number, (i, at) in enumerate(pieces):
        loads.append(
            pltpu.make_async_copy(piece(sources, i, at), piece(held, i, at), in_sem.at[number])
        )
        loads[-1].start()
    for number, (i, at) in enumerate(pieces):
        loads[number].wait()
        stores.append(
            pltpu.make_async_copy(piece(held, i, at), piece(targets, i, at), out_sem.at[number])
        )
        stores[-1].start()
    for store in stores:
        store.wait()


def per_device(
    master, moment_one, moment_two, gradients, norm_gain, hidden_in, expert_ids, route_weights
):
    smem = pl.BlockSpec(memory_space=pltpu.SMEM)
    anywhere = pl.BlockSpec(memory_space=pltpu.HBM)
    flat = (384, PART)
    dma = pltpu.SemaphoreType.DMA
    out_shape = (
        jax.ShapeDtypeStruct(flat, F32),
        jax.ShapeDtypeStruct(flat, F32),
        jax.ShapeDtypeStruct(flat, F32),
        jax.ShapeDtypeStruct((3, 128, WIDTH), BF16),
        jax.ShapeDtypeStruct((4, 4, WIDTH), BF16),
    )
    results = pl.pallas_call(
        body,
        out_shape=out_shape,
        in_specs=[smem, smem] + [anywhere] * 6,
        out_specs=(anywhere,) * 5,
        scratch_shapes=[
            pltpu.VMEM(flat, F32),
            pltpu.VMEM(flat, F32),
            pltpu.VMEM(flat, F32),
            pltpu.VMEM((4, 4, WIDTH), BF16),
            pltpu.VMEM(flat, F32),
            pltpu.VMEM(flat, F32),
            pltpu.VMEM(flat, F32),
            pltpu.VMEM(flat, BF16),
            pltpu.VMEM((1, WIDTH), F32),
            pltpu.VMEM((4, 4, WIDTH), BF16),
            pltpu.VMEM((16, WIDTH), F32),
            pltpu.VMEM((2, 4, 8, WIDTH), BF16),
            pltpu.VMEM((4, 8, 128), F32),
            pltpu.VMEM((4, 8, 128), F32),
            pltpu.VMEM((22, 8, 128), F32),
            pltpu.VMEM((3, 2, BLOCK, WIDTH), BF16),
            pltpu.VMEM((5, 4, BLOCK, WIDTH), BF16),
            pltpu.VMEM((2, 4, 4, 16, WIDTH), BF16),
            pltpu.VMEM((2, 2, 4, 16, WIDTH), BF16),
            pltpu.VMEM((2, 4, 16, WIDTH), BF16),
            pltpu.VMEM((2, 2, 4, 16, WIDTH), BF16),
            pltpu.VMEM((2, 4, 2, 16, WIDTH), BF16),
            pltpu.VMEM((2, 4, 8, WIDTH), BF16),
            pltpu.VMEM((2, 3, 8, WIDTH), BF16),
            pltpu.VMEM((3, 4, 32, PART), BF16),
            pltpu.VMEM((3, 4, 32, PART), BF16),
            pltpu.VMEM((3, 4, 32, PART), BF16),
            pltpu.VMEM((3, 4, 32, PART), BF16),
            pltpu.VMEM((3, 4, 32, PART), BF16),
            pltpu.VMEM((2, 3, 128, WIDTH), BF16),
            dma((6,)),
            dma((5,)),
            dma((2, 22)),
            dma((2, 3)),
            dma((2, 3)),
            dma((2, 3)),
            dma((2, 4)),
            dma((2, 2, 4)),
            dma((2, 2, 3)),
            dma((2, 2, 4)),
            dma((2, 2, 3)),
            dma((2, 3, 3)),
            dma((2, 3, 3)),
            dma((2, 3, 3)),
            dma((2, 3, 3)),
            dma((2, 3, 4)),
            dma((2, 3, 8)),
        ],
        compiler_params=pltpu.CompilerParams(
            collective_id=0, has_side_effects=True, vmem_limit_bytes=56 * 1024 * 1024
        ),
        name="step",
    )(
        expert_ids.transpose(0, 2, 1),
        route_weights.transpose(0, 2, 1),
        master.reshape(flat),
        moment_one.reshape(flat),
        moment_two.reshape(flat),
        gradients.reshape(flat),
        norm_gain.reshape(1, WIDTH),
        hidden_in,
    )
    new_master, new_one, new_two, served, decoded = pl.pallas_call(
        hand_out,
        out_shape=out_shape,
        in_specs=[anywhere] * 5,
        out_specs=(anywhere,) * 5,
        scratch_shapes=[pltpu.VMEM(array.shape, array.dtype) for array in out_shape]
        + [dma((7,)), dma((7,))],
        name="hand_out",
    )(*results)
    return (
        new_master.reshape(master.shape),
        new_one.reshape(master.shape),
        new_two.reshape(master.shape),
        served,
        decoded,
    )


def solution(mesh):
    split = Mesh(mesh.devices.reshape(4, 4, 4, 4, 2), DP_TENSOR)
    sharded = P(None, None, DP, TENSOR)
    by_row = P(None, DP_TENSOR, None)
    return jax.shard_map(
        per_device,
        mesh=split,
        in_specs=(sharded, sharded, sharded, sharded, P(), by_row, by_row, by_row),
        out_specs=(sharded, sharded, sharded, P(None, DP, None), by_row),
        check_vma=False,
    )
```

```python
import math

import jax
import jax.numpy as jnp
from jax import lax
from jax.experimental import pallas as pl
from jax.experimental.pallas import tpu as pltpu
from jax.sharding import Mesh
from jax.sharding import PartitionSpec as P

DP = ("dp_0", "dp_1", "dp_2")
TENSOR = ("tensor_0", "tensor_1")
DP_TENSOR = DP + TENSOR
X_AXIS, Y_AXIS, ZH_AXIS, ZL_AXIS, C_AXIS = DP_TENSOR

MESH = pl.DeviceIdType.MESH
F32 = jnp.float32
BF16 = jnp.bfloat16

beta_one = 0.9
beta_two = 0.95
learn_rate = 0.02
decay_rate = 0.1
adam_eps = 1e-08
step_count = 10
norm_eps = 1e-06

WIDTH = 2048
PART = 256
HIDDEN = 1024
COUNT = 3 * 8 * 1024 * 2048
BLOCK = 32


def one_hot_rows(source_of):
    row = lax.broadcasted_iota(jnp.int32, (128, 128), 0)
    column = lax.broadcasted_iota(jnp.int32, (128, 128), 1)
    a, b, c, i = row // 32, (row // 8) % 4, (row // 2) % 4, row % 2
    return jnp.where(column == source_of(a, b, c, i), 1.0, 0.0).astype(BF16)


def matmul(left, right):
    return lax.dot_general(left, right, (((1,), (0,)), ((), ())), preferred_element_type=F32)


def matmul_nt(left, right):
    return lax.dot_general(left, right, (((1,), (1,)), ((), ())), preferred_element_type=F32)


def body(
    ids_ref,
    gates_ref,
    master_hbm,
    one_hbm,
    two_hbm,
    grad_hbm,
    gain_hbm,
    hidden_hbm,
    new_master_hbm,
    new_one_hbm,
    new_two_hbm,
    served_hbm,
    decoded_hbm,
    new_master_ref,
    new_one_ref,
    new_two_ref,
    decoded_ref,
    master_ref,
    one_ref,
    two_ref,
    grad_ref,
    gain_ref,
    hidden_ref,
    wide,
    zrows,
    meta,
    sums_out,
    sums_in,
    stage,
    slots,
    answers,
    from_core,
    relay,
    joined,
    back,
    parts,
    parts_in,
    wz_out,
    wz_in,
    wy_out,
    wy_in,
    wx_out,
    wall,
    in_sem,
    out_sem,
    sum_sem,
    meta_sem,
    tok_sem,
    x_sem,
    y_sem,
    core_sem,
    ret_sem,
    turn_sem,
    back_sem,
    end_sem,
    wz_sem,
    wy_sem,
    wx_sem,
    wl_sem,
    wc_sem,
    wp_sem,
):
    x = lax.axis_index(X_AXIS)
    y = lax.axis_index(Y_AXIS)
    zh = lax.axis_index(ZH_AXIS)
    zl = lax.axis_index(ZL_AXIS)
    core = lax.axis_index(C_AXIS)
    pair = y // 2
    odd = y % 2
    partner = y + 1 - 2 * odd
    other = (y + 3 + 2 * odd) % 4
    next_core = {C_AXIS: 1 - core}
    started = []

    def send(source, target, sems, index, device):
        copy = pltpu.make_async_remote_copy(
            src_ref=source,
            dst_ref=target,
            send_sem=sems.at[(0,) + index],
            recv_sem=sems.at[(1,) + index],
            device_id=device,
            device_id_type=MESH,
        )
        copy.start()
        started.append(copy)
        return copy

    def turn(axis, me, j):
        return {axis: (me + j) % 4}

    def along_z(j):
        z = (4 * zh + zl + j) % 16
        return {ZH_AXIS: z // 4, ZL_AXIS: z % 4}

    barrier = pltpu.get_barrier_semaphore()
    peers = [along_z(j) for j in (8, 7, 9, 6, 10, 5, 11, 4, 12, 3, 13, 2, 14, 1, 15)]
    peers += [turn(axis, me, j) for axis, me in ((X_AXIS, x), (Y_AXIS, y)) for j in (2, 1, 3)]
    peers += [{Y_AXIS: partner, C_AXIS: 1 - core}, next_core]
    for peer in peers:
        pl.semaphore_signal(barrier, inc=1, device_id=peer, device_id_type=MESH)
    loads = [
        pltpu.make_async_copy(source, target, in_sem.at[number])
        for number, (source, target) in enumerate(
            (
                (hidden_hbm, hidden_ref),
                (gain_hbm, gain_ref),
                (grad_hbm, grad_ref),
                (master_hbm, master_ref),
                (one_hbm, one_ref),
                (two_hbm, two_ref),
            )
        )
    ]
    for load in loads:
        load.start()

    meta_row = lax.broadcasted_iota(jnp.int32, (8, 128), 0)
    meta_lane = lax.broadcasted_iota(jnp.int32, (8, 128), 1) - zh * 16
    tile = jnp.zeros((8, 128), F32)
    for s in range(4):
        for r in range(4):
            spot = meta_lane == 4 * s + r
            for k in range(2):
                tile = jnp.where(spot & (meta_row == k), ids_ref[s, k, r].astype(F32), tile)
                tile = jnp.where(spot & (meta_row == 2 + k), gates_ref[s, k, r], tile)
    meta[0] = tile
    loads[0].wait()
    loads[1].wait()
    for s in range(4):
        wide[pl.ds(4 * s, 4), :] = hidden_ref[s].astype(F32)
    rows = wide[...]
    factor = lax.rsqrt(jnp.mean(rows * rows, axis=1, keepdims=True) + norm_eps)
    normed = rows * factor * gain_ref[...]
    zrows[zh] = normed.astype(BF16)
    loads[2].wait()
    squares = jnp.zeros((8, 128), F32)
    for block in range(12):
        values = grad_ref[pl.ds(32 * block, 32), :].astype(F32)
        values = values * values
        for i in range(4):
            for h in range(2):
                squares = squares + values[8 * i : 8 * i + 8, 128 * h : 128 * h + 128]
    sums_out[0] = squares
    pl.semaphore_wait(barrier, len(peers))

    slot = 0
    token_copies = []
    for phase, devices in enumerate(
        (
            [along_z(j) for j in (8, 7, 9, 6, 10, 5, 11, 4, 12, 3, 13, 2, 14, 1, 15)],
            [turn(X_AXIS, x, j) for j in (2, 1, 3)],
            [turn(Y_AXIS, y, j) for j in (2, 1, 3)],
            [next_core],
        )
    ):
        copies = [
            send(sums_out.at[phase], sums_in.at[slot + i], sum_sem, (slot + i,), device)
            for i, device in enumerate(devices)
        ]
        if phase == 0:
            for j in (2, 1, 3):
                token_copies.append(
                    send(meta.at[0], meta.at[j], meta_sem, (j - 1,), turn(ZH_AXIS, zh, j))
                )
                token_copies.append(
                    send(zrows.at[zh], zrows.at[zh], tok_sem, (j - 1,), turn(ZH_AXIS, zh, j))
                )
        if phase == 3:
            permute_z = one_hot_rows(lambda a, b, c, i: ((b * 4 + c) * 4 + a) * 2 + i)
            permute_y = one_hot_rows(lambda a, b, c, i: ((c * 4 + b) * 4 + a) * 2 + i)
            permute_x = one_hot_rows(lambda a, b, c, i: ((b * 4 + a) * 4 + c) * 2 + i)
            for load in loads[3:]:
                load.wait()
        for i, copy in enumerate(copies):
            copy.wait_recv()
            squares = squares + sums_in[slot + i]
        slot += len(copies)
        if phase < 3:
            sums_out[phase + 1] = squares
    total = jnp.sum(squares, axis=(0, 1), keepdims=True)
    clip = jnp.minimum(1.0, lax.rsqrt(total * (1.0 / COUNT) + norm_eps))

    first_fix = 1.0 / (1.0 - beta_one**step_count)
    second_fix = 1.0 / (1.0 - beta_two**step_count)
    z_copies = []
    stores = []

    def keep(source, target):
        copy = pltpu.make_async_copy(source, target, out_sem.at[len(stores)])
        copy.start()
        stores.append(copy)

    for k in range(3):
        for block in range(4):
            at = pl.ds(128 * k + 32 * block, 32)
            scaled = grad_ref[at, :].astype(F32) * clip
            first = beta_one * one_ref[at, :] + (1.0 - beta_one) * scaled
            second = beta_two * two_ref[at, :] + (1.0 - beta_two) * scaled * scaled
            update = first * first_fix / (jnp.sqrt(second * second_fix) + adam_eps)
            old = master_ref[at, :]
            new_master_ref[at, :] = old - learn_rate * (update + decay_rate * old)
            new_one_ref[at, :] = first
            new_two_ref[at, :] = second
        rounded = new_master_ref[pl.ds(128 * k, 128), :].astype(BF16)
        wz_out[k] = matmul(permute_z, rounded).astype(BF16).reshape(4, 32, PART)
        for j in (2, 1, 3):
            z_copies.append(
                send(
                    wz_out.at[k, (zh + j) % 4],
                    wz_in.at[k, zh],
                    wz_sem,
                    (k, j - 1),
                    turn(ZH_AXIS, zh, j),
                )
            )
        wz_in[k, zh] = wz_out[k, zh]
    keep(new_master_ref, new_master_hbm)
    keep(new_one_ref, new_one_hbm)
    keep(new_two_ref, new_two_hbm)

    for copy in token_copies:
        copy.wait_recv()
    routes = meta[0] + meta[1] + meta[2] + meta[3]
    id_one, id_two = routes[0:1, 0:64], routes[1:2, 0:64]
    gate_one, gate_two = routes[2:3, 0:64], routes[3:4, 0:64]
    gate_sum = gate_one + gate_two
    share_one, share_two = gate_one / gate_sum, gate_two / gate_sum
    place = lax.broadcasted_iota(jnp.int32, (8, 64), 0)
    expert = (2 * ((x + place // 2) % 4) + (pair + place % 2) % 2).astype(F32)
    names_one = jnp.where(id_one == expert, 1.0, 0.0)
    names_two = jnp.where(id_two == expert, 1.0, 0.0)
    named = names_one + names_two
    share = names_one * share_one + names_two * share_two
    above = lax.broadcasted_iota(jnp.int32, (64, 64), 0)
    below = lax.broadcasted_iota(jnp.int32, (64, 64), 1)
    before = jnp.where((above // 4 == below // 4) & (above < below), 1.0, 0.0).astype(BF16)
    earlier = matmul(named.astype(BF16), before)
    slot_row = lax.broadcasted_iota(jnp.int32, (32, 64), 0)
    row_lane = lax.broadcasted_iota(jnp.int32, (32, 64), 1)
    same_block = jnp.where(
        (slot_row // 8 == (row_lane // 4) % 4) & ((slot_row // 2) % 4 == row_lane // 16), 1.0, 0.0
    )
    slot_number = (slot_row % 2).astype(F32)
    hits = [jnp.where(earlier[p : p + 1, :] == slot_number, same_block, 0.0) for p in range(8)]
    token_rows = zrows[...].reshape(64, WIDTH)
    x_copies = {}
    for d in (0, 2, 1, 3):
        picks = [hits[2 * d + r] * named[2 * d + r : 2 * d + r + 1, :] for r in (1, 0)]
        chosen = matmul(jnp.concatenate(picks, axis=0).astype(BF16), token_rows)
        chosen = chosen.astype(BF16).reshape(2, BLOCK, WIDTH)
        if d == 0:
            slots[0, 0] = chosen[0]
            slots[1, 0] = chosen[1]
        else:
            stage[d - 1] = chosen
            x_copies[d] = send(
                stage.at[d - 1], slots.at[pl.ds(0, 2), d], x_sem, (d - 1,), turn(X_AXIS, x, d)
            )
    weights = []
    for s in range(4):
        columns = [(hits[p] * share[p : p + 1, :])[8 * s : 8 * s + 8] for p in range(8)]
        weight = jnp.concatenate(columns, axis=0).T
        weight = jnp.concatenate([weight[16 * i + 4 * s : 16 * i + 4 * s + 4] for i in range(4)])
        high = weight.astype(BF16)
        rest = weight - high.astype(F32)
        middle = rest.astype(BF16)
        low = (rest - middle.astype(F32)).astype(BF16)
        weights.append(jnp.concatenate([high, middle, low], axis=0))

    over_y, over_core = {}, []

    def spread(d):
        if d:
            x_copies[d].wait_recv()
        over_y[d] = send(slots.at[0, d], slots.at[3, d], y_sem, (d,), {Y_AXIS: other})
        over_core.append(send(slots.at[1, d], slots.at[2, d], core_sem, (0, d), next_core))

    def forward(d):
        over_y[d].wait_recv()
        over_core.append(send(slots.at[3, d], slots.at[4, d], core_sem, (1, d), next_core))

    def columns_of(position):
        return pl.ds(pl.multiple_of((2 * position + core) * PART, PART), PART)

    own_rows = pl.ds(pl.multiple_of(32 * x, 32), 32)
    across = {Y_AXIS: partner, C_AXIS: odd}
    y_copies, wx_copies, core_copies, line_sends = {}, {}, {0: [], 1: [], 2: []}, []

    def over_wy(k):
        for copy in z_copies[3 * k : 3 * k + 3]:
            copy.wait_recv()
        gathered = wz_in[k].reshape(128, PART)
        wy_out[k] = matmul(permute_y, gathered).astype(BF16).reshape(4, 32, PART)
        y_copies[k] = [
            send(wy_out.at[k, (y + j) % 4], wy_in.at[k, y], wy_sem, (k, j - 1), turn(Y_AXIS, y, j))
            for j in (2, 1, 3)
        ]
        wy_in[k, y] = wy_out[k, y]

    def over_wx(k):
        for copy in y_copies[k]:
            copy.wait_recv()
        gathered = wy_in[k].reshape(128, PART)
        wx_out[k] = matmul(permute_x, gathered).astype(BF16).reshape(4, 32, PART)
        wx_copies[k] = [
            send(
                wx_out.at[k, (x + j) % 4],
                wall.at[odd, k, own_rows, columns_of(zl)],
                wx_sem,
                (k, j - 1),
                turn(X_AXIS, x, j),
            )
            for j in (2, 1, 3)
        ]
        wall[odd, k, own_rows, columns_of(zl)] = wx_out[k, x]

    def line_copy(k, position, number, arrival, target):
        piece = wall.at[odd, k, :, columns_of(position)]
        return pltpu.make_async_remote_copy(
            src_ref=piece,
            dst_ref=piece,
            send_sem=wl_sem.at[0, k, number],
            recv_sem=wl_sem.at[1, k, arrival],
            device_id={ZL_AXIS: target},
            device_id_type=MESH,
        )

    def line_send(copy, wanted):
        @pl.when(wanted)
        def _():
            copy.start()

        line_sends.append((copy, wanted))

    def share_out(k, j, position):
        piece = wall.at[odd, k, :, columns_of(position)]
        send(piece, piece, wp_sem, (k, 2 * j + core), across)
        core_copies[k].append(send(piece, piece, wc_sem, (k, j), next_core))

    def over_line(k):
        for copy in wx_copies[k]:
            copy.wait_recv()
        for j in (2, 1, 3):
            near = True if j == 2 else (zl != (3 if j == 1 else 0))
            line_send(line_copy(k, zl, j - 1, j - 1, (zl + j) % 4), near)
        share_out(k, 0, zl)

    late = jnp.where(zl == 0, 1, 3)
    relay_to = jnp.where(zl == 2, 3, 0)

    def onward(k):
        for j in (2, 4 - late, late):
            position = (zl + 4 - j) % 4
            line_copy(k, position, j - 1, j - 1, zl).wait_recv()
            if isinstance(j, int):
                relayed = line_copy(k, position, 3, jnp.where(zl == 2, 2, 0), relay_to)
                line_send(relayed, (zl == 1) | (zl == 2))
            share_out(k, j, position)

    over_wy(0)
    over_wy(1)
    over_wx(0)
    over_wy(2)
    over_wx(1)
    over_line(0)
    spread(0)
    over_wx(2)
    over_line(1)
    spread(1)
    forward(0)
    over_line(2)
    onward(0)
    spread(3)
    forward(1)
    onward(1)
    spread(2)
    forward(3)
    onward(2)
    forward(2)

    def wait_weights(k):
        for copy in core_copies[k]:
            copy.wait_recv()

        @pl.when(core != odd)
        def _():
            for number in range(8):
                piece = wall.at[core, k, :, pl.ds(PART * number, PART)]
                pltpu.make_async_remote_copy(
                    src_ref=piece,
                    dst_ref=piece,
                    send_sem=wp_sem.at[0, k, number],
                    recv_sem=wp_sem.at[1, k, number],
                    device_id=across,
                    device_id_type=MESH,
                ).wait_recv()

    for copy in over_core:
        copy.wait_recv()
    wait_weights(0)
    wait_weights(1)

    into = wall.at[core, pl.ds(0, 2)]
    active = []
    for h in range(2):
        taken = slots[pl.ds(1, 4), :, pl.ds(16 * h, 16), :].reshape(256, WIDTH)
        projected = matmul_nt(taken, into[...].reshape(256, WIDTH)) * (1.0 / math.sqrt(WIDTH))
        gate, up = projected[:, :128], projected[:, 128:]
        active.append((gate / (1.0 + jnp.exp(-gate)) * up).astype(BF16))
    wait_weights(2)
    keep(wall.at[odd], served_hbm)
    swaps = []
    for h in range(2):
        for i in range(4):
            span = pl.ds(512 * i, 512)
            out = matmul(active[h], wall[core, 2, :, span]) * (1.0 / math.sqrt(HIDDEN))
            out = out.reshape(4, 4, 16, 512)
            answers[2 * h, :, :, :, span] = out[:, :, 0:8].astype(BF16)
            answers[2 * h + 1, :, :, :, span] = out[:, :, 8:16].astype(BF16)
        for s in (2 * h, 2 * h + 1):
            for number in (3, 1):
                swaps.append(
                    send(
                        answers.at[s, number],
                        from_core.at[s, number // 2],
                        ret_sem,
                        (s, number // 2),
                        next_core,
                    )
                )

    over_y = []
    for s in range(4):
        swaps[2 * s].wait_recv()
        relay[s] = (answers[s, 2].astype(F32) + from_core[s, 1].astype(F32)).astype(BF16)
        over_y.append(send(relay.at[s], joined.at[s, 1], turn_sem, (s,), {Y_AXIS: other}))
    for s in range(4):
        swaps[2 * s + 1].wait_recv()
        joined[s, 0] = (answers[s, 0].astype(F32) + from_core[s, 0].astype(F32)).astype(BF16)

    over_x, over_z = {}, {}

    def along_x(s):
        over_y[s].wait_recv()
        over_x[s] = [
            send(joined.at[s, :, d], back.at[s, d], back_sem, (s, d), turn(X_AXIS, x, 4 - d))
            for d in (2, 1, 3)
        ]
        back[s, 0] = joined[s, :, 0]

    def to_rows(s):
        for copy in over_x[s]:
            copy.wait_recv()
        made = matmul(weights[s], back[s].reshape(64, WIDTH))
        made = made[0:16] + made[16:32] + made[32:48]
        for i in range(4):
            parts[s, i] = made[4 * i : 4 * i + 4].astype(BF16)
        over_z[s] = [
            send(
                parts.at[s, (zh + j) % 4],
                parts_in.at[s, j - 1],
                end_sem,
                (s, j - 1),
                turn(ZH_AXIS, zh, j),
            )
            for j in (2, 1, 3)
        ]

    along_x(0)
    along_x(1)
    to_rows(0)
    along_x(2)
    to_rows(1)
    along_x(3)
    to_rows(2)
    to_rows(3)
    for s in range(4):
        result = wide[pl.ds(4 * s, 4), :] + parts[s, zh].astype(F32)
        for copy in over_z[s]:
            copy.wait_recv()
        for j in range(3):
            result = result + parts_in[s, j].astype(F32)
        decoded_ref[s] = result.astype(BF16)
    keep(decoded_ref, decoded_hbm)
    for copy in stores:
        copy.wait()
    for copy in started:
        copy.wait_send()
    for copy, wanted in line_sends:

        @pl.when(wanted)
        def _(copy=copy):
            copy.wait_send()


def hand_out(*refs):
    sources, targets, held, in_sem, out_sem = refs[:5], refs[5:10], refs[10:15], refs[15], refs[16]
    pieces = [(i, ()) for i in (0, 1, 2)] + [(3, (k,)) for k in range(3)] + [(4, ())]

    def piece(refs, i, at):
        return refs[i].at[at] if at else refs[i]

    loads, stores = [], []
    for number, (i, at) in enumerate(pieces):
        loads.append(
            pltpu.make_async_copy(piece(sources, i, at), piece(held, i, at), in_sem.at[number])
        )
        loads[-1].start()
    for number, (i, at) in enumerate(pieces):
        loads[number].wait()
        stores.append(
            pltpu.make_async_copy(piece(held, i, at), piece(targets, i, at), out_sem.at[number])
        )
        stores[-1].start()
    for store in stores:
        store.wait()


def per_device(
    master, moment_one, moment_two, gradients, norm_gain, hidden_in, expert_ids, route_weights
):
    smem = pl.BlockSpec(memory_space=pltpu.SMEM)
    anywhere = pl.BlockSpec(memory_space=pltpu.HBM)
    flat = (384, PART)
    dma = pltpu.SemaphoreType.DMA
    out_shape = (
        jax.ShapeDtypeStruct(flat, F32),
        jax.ShapeDtypeStruct(flat, F32),
        jax.ShapeDtypeStruct(flat, F32),
        jax.ShapeDtypeStruct((3, 128, WIDTH), BF16),
        jax.ShapeDtypeStruct((4, 4, WIDTH), BF16),
    )
    results = pl.pallas_call(
        body,
        out_shape=out_shape,
        in_specs=[smem, smem] + [anywhere] * 6,
        out_specs=(anywhere,) * 5,
        scratch_shapes=[
            pltpu.VMEM(flat, F32),
            pltpu.VMEM(flat, F32),
            pltpu.VMEM(flat, F32),
            pltpu.VMEM((4, 4, WIDTH), BF16),
            pltpu.VMEM(flat, F32),
            pltpu.VMEM(flat, F32),
            pltpu.VMEM(flat, F32),
            pltpu.VMEM(flat, BF16),
            pltpu.VMEM((1, WIDTH), F32),
            pltpu.VMEM((4, 4, WIDTH), BF16),
            pltpu.VMEM((16, WIDTH), F32),
            pltpu.VMEM((4, 16, WIDTH), BF16),
            pltpu.VMEM((4, 8, 128), F32),
            pltpu.VMEM((4, 8, 128), F32),
            pltpu.VMEM((22, 8, 128), F32),
            pltpu.VMEM((3, 2, BLOCK, WIDTH), BF16),
            pltpu.VMEM((5, 4, BLOCK, WIDTH), BF16),
            pltpu.VMEM((4, 4, 4, 8, WIDTH), BF16),
            pltpu.VMEM((4, 2, 4, 8, WIDTH), BF16),
            pltpu.VMEM((4, 4, 8, WIDTH), BF16),
            pltpu.VMEM((4, 2, 4, 8, WIDTH), BF16),
            pltpu.VMEM((4, 4, 2, 8, WIDTH), BF16),
            pltpu.VMEM((4, 4, 4, WIDTH), BF16),
            pltpu.VMEM((4, 3, 4, WIDTH), BF16),
            pltpu.VMEM((3, 4, 32, PART), BF16),
            pltpu.VMEM((3, 4, 32, PART), BF16),
            pltpu.VMEM((3, 4, 32, PART), BF16),
            pltpu.VMEM((3, 4, 32, PART), BF16),
            pltpu.VMEM((3, 4, 32, PART), BF16),
            pltpu.VMEM((2, 3, 128, WIDTH), BF16),
            dma((6,)),
            dma((5,)),
            dma((2, 22)),
            dma((2, 3)),
            dma((2, 3)),
            dma((2, 3)),
            dma((2, 4)),
            dma((2, 2, 4)),
            dma((2, 4, 2)),
            dma((2, 4)),
            dma((2, 4, 4)),
            dma((2, 4, 3)),
            dma((2, 3, 3)),
            dma((2, 3, 3)),
            dma((2, 3, 3)),
            dma((2, 3, 4)),
            dma((2, 3, 4)),
            dma((2, 3, 8)),
        ],
        compiler_params=pltpu.CompilerParams(
            collective_id=0, has_side_effects=True, vmem_limit_bytes=56 * 1024 * 1024
        ),
        name="step",
    )(
        expert_ids.transpose(0, 2, 1),
        route_weights.transpose(0, 2, 1),
        master.reshape(flat),
        moment_one.reshape(flat),
        moment_two.reshape(flat),
        gradients.reshape(flat),
        norm_gain.reshape(1, WIDTH),
        hidden_in,
    )
    new_master, new_one, new_two, served, decoded = pl.pallas_call(
        hand_out,
        out_shape=out_shape,
        in_specs=[anywhere] * 5,
        out_specs=(anywhere,) * 5,
        scratch_shapes=[pltpu.VMEM(array.shape, array.dtype) for array in out_shape]
        + [dma((7,)), dma((7,))],
        name="hand_out",
    )(*results)
    return (
        new_master.reshape(master.shape),
        new_one.reshape(master.shape),
        new_two.reshape(master.shape),
        served,
        decoded,
    )


def solution(mesh):
    split = Mesh(mesh.devices.reshape(4, 4, 4, 4, 2), DP_TENSOR)
    sharded = P(None, None, DP, TENSOR)
    by_row = P(None, DP_TENSOR, None)
    return jax.shard_map(
        per_device,
        mesh=split,
        in_specs=(sharded, sharded, sharded, sharded, P(), by_row, by_row, by_row),
        out_specs=(sharded, sharded, sharded, P(None, DP, None), by_row),
        check_vma=False,
    )
```

```python
import math

import jax
import jax.numpy as jnp
from jax import lax
from jax.experimental import pallas as pl
from jax.experimental.pallas import tpu as pltpu
from jax.sharding import Mesh
from jax.sharding import PartitionSpec as P

DP = ("dp_0", "dp_1", "dp_2")
TENSOR = ("tensor_0", "tensor_1")
DP_TENSOR = DP + TENSOR
X_AXIS, Y_AXIS, ZH_AXIS, ZL_AXIS, C_AXIS = DP_TENSOR

MESH = pl.DeviceIdType.MESH
F32 = jnp.float32
BF16 = jnp.bfloat16

beta_one = 0.9
beta_two = 0.95
learn_rate = 0.02
decay_rate = 0.1
adam_eps = 1e-08
step_count = 10
norm_eps = 1e-06

WIDTH = 2048
PART = 256
HIDDEN = 1024
COUNT = 3 * 8 * 1024 * 2048
BLOCK = 32


def one_hot_rows(source_of):
    row = lax.broadcasted_iota(jnp.int32, (128, 128), 0)
    column = lax.broadcasted_iota(jnp.int32, (128, 128), 1)
    a, b, c, i = row // 32, (row // 8) % 4, (row // 2) % 4, row % 2
    return jnp.where(column == source_of(a, b, c, i), 1.0, 0.0).astype(BF16)


def matmul(left, right):
    return lax.dot_general(left, right, (((1,), (0,)), ((), ())), preferred_element_type=F32)


def matmul_nt(left, right):
    return lax.dot_general(left, right, (((1,), (1,)), ((), ())), preferred_element_type=F32)


def body(
    ids_ref,
    gates_ref,
    master_hbm,
    one_hbm,
    two_hbm,
    grad_hbm,
    gain_hbm,
    hidden_hbm,
    new_master_hbm,
    new_one_hbm,
    new_two_hbm,
    served_hbm,
    decoded_hbm,
    new_master_ref,
    new_one_ref,
    new_two_ref,
    decoded_ref,
    master_ref,
    one_ref,
    two_ref,
    grad_ref,
    gain_ref,
    hidden_ref,
    wide,
    zrows,
    meta,
    sums_out,
    sums_in,
    stage,
    slots,
    answers,
    from_core,
    relay,
    joined,
    back,
    parts,
    parts_in,
    wz_out,
    wz_in,
    wy_out,
    wy_in,
    wx_out,
    wall,
    active,
    in_sem,
    out_sem,
    sum_sem,
    meta_sem,
    tok_sem,
    x_sem,
    y_sem,
    core_sem,
    ret_sem,
    turn_sem,
    back_sem,
    end_sem,
    wz_sem,
    wy_sem,
    wx_sem,
    wl_sem,
    wc_sem,
    wp_sem,
):
    x = lax.axis_index(X_AXIS)
    y = lax.axis_index(Y_AXIS)
    zh = lax.axis_index(ZH_AXIS)
    zl = lax.axis_index(ZL_AXIS)
    core = lax.axis_index(C_AXIS)
    pair = y // 2
    odd = y % 2
    partner = y + 1 - 2 * odd
    other = (y + 3 + 2 * odd) % 4
    next_core = {C_AXIS: 1 - core}
    started = []

    def send(source, target, sems, index, device):
        copy = pltpu.make_async_remote_copy(
            src_ref=source,
            dst_ref=target,
            send_sem=sems.at[(0,) + index],
            recv_sem=sems.at[(1,) + index],
            device_id=device,
            device_id_type=MESH,
        )
        copy.start()
        started.append(copy)
        return copy

    def turn(axis, me, j):
        return {axis: (me + j) % 4}

    def along_z(j):
        z = (4 * zh + zl + j) % 16
        return {ZH_AXIS: z // 4, ZL_AXIS: z % 4}

    barrier = pltpu.get_barrier_semaphore()
    peers = [along_z(j) for j in (8, 7, 9, 6, 10, 5, 11, 4, 12, 3, 13, 2, 14, 1, 15)]
    peers += [turn(axis, me, j) for axis, me in ((X_AXIS, x), (Y_AXIS, y)) for j in (2, 1, 3)]
    peers += [{Y_AXIS: partner, C_AXIS: 1 - core}, next_core]
    for peer in peers:
        pl.semaphore_signal(barrier, inc=1, device_id=peer, device_id_type=MESH)
    loads = [
        pltpu.make_async_copy(source, target, in_sem.at[number])
        for number, (source, target) in enumerate(
            (
                (hidden_hbm, hidden_ref),
                (gain_hbm, gain_ref),
                (grad_hbm, grad_ref),
                (master_hbm, master_ref),
                (one_hbm, one_ref),
                (two_hbm, two_ref),
            )
        )
    ]
    for load in loads:
        load.start()

    meta_row = lax.broadcasted_iota(jnp.int32, (8, 128), 0)
    meta_lane = lax.broadcasted_iota(jnp.int32, (8, 128), 1) - zh * 16
    tile = jnp.zeros((8, 128), F32)
    for s in range(4):
        for r in range(4):
            spot = meta_lane == 4 * s + r
            for k in range(2):
                tile = jnp.where(spot & (meta_row == k), ids_ref[s, k, r].astype(F32), tile)
                tile = jnp.where(spot & (meta_row == 2 + k), gates_ref[s, k, r], tile)
    meta[0] = tile[0:4]
    loads[0].wait()
    loads[1].wait()
    for s in range(4):
        wide[pl.ds(4 * s, 4), :] = hidden_ref[s].astype(F32)
    rows = wide[...]
    factor = lax.rsqrt(jnp.mean(rows * rows, axis=1, keepdims=True) + norm_eps)
    normed = rows * factor * gain_ref[...]
    zrows[zh] = normed.astype(BF16)
    loads[2].wait()

    def add_block(block, squares):
        values = grad_ref[pl.ds(pl.multiple_of(32 * block, 32), 32), :].astype(F32)
        values = values * values
        for i in range(4):
            for h in range(2):
                squares = squares + values[8 * i : 8 * i + 8, 128 * h : 128 * h + 128]
        return squares

    squares = lax.fori_loop(0, 12, add_block, jnp.zeros((8, 128), F32))
    squares = jnp.sum(squares, axis=0, keepdims=True)
    sums_out[0] = squares
    pl.semaphore_wait(barrier, len(peers))

    slot = 0
    token_copies = []
    for phase, devices in enumerate(
        (
            [along_z(j) for j in (8, 7, 9, 6, 10, 5, 11, 4, 12, 3, 13, 2, 14, 1, 15)],
            [turn(X_AXIS, x, j) for j in (2, 1, 3)],
            [turn(Y_AXIS, y, j) for j in (2, 1, 3)],
            [next_core],
        )
    ):
        copies = [
            send(sums_out.at[phase], sums_in.at[slot + i], sum_sem, (slot + i,), device)
            for i, device in enumerate(devices)
        ]
        if phase == 0:
            for j in (2, 1, 3):
                token_copies.append(
                    send(meta.at[0], meta.at[j], meta_sem, (j - 1,), turn(ZH_AXIS, zh, j))
                )
                token_copies.append(
                    send(zrows.at[zh], zrows.at[zh], tok_sem, (j - 1,), turn(ZH_AXIS, zh, j))
                )
        if phase == 3:
            permute_z = one_hot_rows(lambda a, b, c, i: ((b * 4 + c) * 4 + a) * 2 + i)
            permute_y = one_hot_rows(lambda a, b, c, i: ((c * 4 + b) * 4 + a) * 2 + i)
            permute_x = one_hot_rows(lambda a, b, c, i: ((b * 4 + a) * 4 + c) * 2 + i)
            for load in loads[3:]:
                load.wait()
        for i, copy in enumerate(copies):
            copy.wait_recv()
            squares = squares + sums_in[slot + i]
        slot += len(copies)
        if phase < 3:
            sums_out[phase + 1] = squares
    total = jnp.sum(squares, axis=(0, 1), keepdims=True)
    clip = jnp.minimum(1.0, lax.rsqrt(total * (1.0 / COUNT) + norm_eps))

    x_copies = {}
    hits = []
    routed = []

    def pick():
        for copy in token_copies:
            copy.wait_recv()
        routes = meta[0] + meta[1] + meta[2] + meta[3]
        id_one, id_two = routes[0:1, 0:64], routes[1:2, 0:64]
        gate_one, gate_two = routes[2:3, 0:64], routes[3:4, 0:64]
        gate_sum = gate_one + gate_two
        share_one, share_two = gate_one / gate_sum, gate_two / gate_sum
        place = lax.broadcasted_iota(jnp.int32, (8, 64), 0)
        expert = (2 * ((x + place // 2) % 4) + (pair + place % 2) % 2).astype(F32)
        names_one = jnp.where(id_one == expert, 1.0, 0.0)
        names_two = jnp.where(id_two == expert, 1.0, 0.0)
        named = names_one + names_two
        share = names_one * share_one + names_two * share_two
        above = lax.broadcasted_iota(jnp.int32, (64, 64), 0)
        below = lax.broadcasted_iota(jnp.int32, (64, 64), 1)
        before = jnp.where((above // 4 == below // 4) & (above < below), 1.0, 0.0).astype(BF16)
        earlier = matmul(named.astype(BF16), before)
        slot_row = lax.broadcasted_iota(jnp.int32, (32, 64), 0)
        row_lane = lax.broadcasted_iota(jnp.int32, (32, 64), 1)
        same_block = jnp.where(
            (slot_row // 8 == (row_lane // 4) % 4) & ((slot_row // 2) % 4 == row_lane // 16), 1.0, 0.0
        )
        slot_number = (slot_row % 2).astype(F32)
        hits[:] = [jnp.where(earlier[p : p + 1, :] == slot_number, same_block, 0.0) for p in range(8)]
        token_rows = zrows[...].reshape(64, WIDTH)
        for d in (0, 2, 1, 3):
            picks = [hits[2 * d + r] * named[2 * d + r : 2 * d + r + 1, :] for r in (1, 0)]
            chosen = matmul(jnp.concatenate(picks, axis=0).astype(BF16), token_rows)
            chosen = chosen.astype(BF16).reshape(2, BLOCK, WIDTH)
            if d == 0:
                slots[0, 0] = chosen[0]
                slots[1, 0] = chosen[1]
            else:
                stage[d - 1] = chosen
                x_copies[d] = send(
                    stage.at[d - 1], slots.at[pl.ds(0, 2), d], x_sem, (d - 1,), turn(X_AXIS, x, d)
                )
        routed.append(share)

    first_fix = 1.0 / (1.0 - beta_one**step_count)
    second_fix = 1.0 / (1.0 - beta_two**step_count)
    z_copies = []
    stores = []

    def keep(source, target):
        copy = pltpu.make_async_copy(source, target, out_sem.at[len(stores)])
        copy.start()
        stores.append(copy)

    for k in range(3):
        @pl.loop(0, 4)
        def _(block, k=k):
            at = pl.ds(pl.multiple_of(128 * k + 32 * block, 32), 32)
            scaled = grad_ref[at, :].astype(F32) * clip
            first = beta_one * one_ref[at, :] + (1.0 - beta_one) * scaled
            second = beta_two * two_ref[at, :] + (1.0 - beta_two) * scaled * scaled
            update = first * first_fix / (jnp.sqrt(second * second_fix) + adam_eps)
            old = master_ref[at, :]
            new_master_ref[at, :] = old - learn_rate * (update + decay_rate * old)
            new_one_ref[at, :] = first
            new_two_ref[at, :] = second

        rounded = new_master_ref[pl.ds(128 * k, 128), :].astype(BF16)
        wz_out[k] = matmul(permute_z, rounded).astype(BF16).reshape(4, 32, PART)
        for j in (2, 1, 3):
            z_copies.append(
                send(
                    wz_out.at[k, (zh + j) % 4],
                    wz_in.at[k, zh],
                    wz_sem,
                    (k, j - 1),
                    turn(ZH_AXIS, zh, j),
                )
            )
        wz_in[k, zh] = wz_out[k, zh]
        if k == 0:
            pick()
    keep(new_master_ref, new_master_hbm)
    keep(new_one_ref, new_one_hbm)
    keep(new_two_ref, new_two_hbm)

    over_y, over_core = {}, []

    def spread(d):
        if d:
            x_copies[d].wait_recv()
        over_y[d] = send(slots.at[0, d], slots.at[3, d], y_sem, (d,), {Y_AXIS: other})
        over_core.append(send(slots.at[1, d], slots.at[2, d], core_sem, (0, d), next_core))

    def forward(d):
        over_y[d].wait_recv()
        over_core.append(send(slots.at[3, d], slots.at[4, d], core_sem, (1, d), next_core))

    def columns_of(position):
        return pl.ds(pl.multiple_of((2 * position + core) * PART, PART), PART)

    own_rows = pl.ds(pl.multiple_of(32 * x, 32), 32)
    across = {Y_AXIS: partner, C_AXIS: odd}
    y_copies, wx_copies, core_copies, line_sends = {}, {}, {0: [], 1: [], 2: []}, []

    def over_wy(k):
        for copy in z_copies[3 * k : 3 * k + 3]:
            copy.wait_recv()
        gathered = wz_in[k].reshape(128, PART)
        wy_out[k] = matmul(permute_y, gathered).astype(BF16).reshape(4, 32, PART)
        y_copies[k] = [
            send(wy_out.at[k, (y + j) % 4], wy_in.at[k, y], wy_sem, (k, j - 1), turn(Y_AXIS, y, j))
            for j in (2, 1, 3)
        ]
        wy_in[k, y] = wy_out[k, y]

    def over_wx(k):
        for copy in y_copies[k]:
            copy.wait_recv()
        gathered = wy_in[k].reshape(128, PART)
        wx_out[k] = matmul(permute_x, gathered).astype(BF16).reshape(4, 32, PART)
        wx_copies[k] = [
            send(
                wx_out.at[k, (x + j) % 4],
                wall.at[odd, k, own_rows, columns_of(zl)],
                wx_sem,
                (k, j - 1),
                turn(X_AXIS, x, j),
            )
            for j in (2, 1, 3)
        ]
        wall[odd, k, own_rows, columns_of(zl)] = wx_out[k, x]

    def line_copy(k, position, number, arrival, target):
        piece = wall.at[odd, k, :, columns_of(position)]
        return pltpu.make_async_remote_copy(
            src_ref=piece,
            dst_ref=piece,
            send_sem=wl_sem.at[0, k, number],
            recv_sem=wl_sem.at[1, k, arrival],
            device_id={ZL_AXIS: target},
            device_id_type=MESH,
        )

    def line_send(copy, wanted):
        @pl.when(wanted)
        def _():
            copy.start()

        line_sends.append((copy, wanted))

    def share_out(k, j, position):
        piece = wall.at[odd, k, :, columns_of(position)]
        send(piece, piece, wp_sem, (k, 2 * j + core), across)
        core_copies[k].append(send(piece, piece, wc_sem, (k, j), next_core))

    def over_line(k):
        for copy in wx_copies[k]:
            copy.wait_recv()
        for j in (2, 1, 3):
            near = True if j == 2 else (zl != (3 if j == 1 else 0))
            line_send(line_copy(k, zl, j - 1, j - 1, (zl + j) % 4), near)
        share_out(k, 0, zl)

    late = jnp.where(zl == 0, 1, 3)
    relay_to = jnp.where(zl == 2, 3, 0)

    def onward(k):
        for j in (2, 4 - late, late):
            position = (zl + 4 - j) % 4
            line_copy(k, position, j - 1, j - 1, zl).wait_recv()
            if isinstance(j, int):
                relayed = line_copy(k, position, 3, jnp.where(zl == 2, 2, 0), relay_to)
                line_send(relayed, (zl == 1) | (zl == 2))
            share_out(k, j, position)

    over_wy(0)
    over_wy(1)
    over_wx(0)
    over_wy(2)
    over_wx(1)
    over_line(0)
    spread(0)
    over_wx(2)
    over_line(1)
    spread(1)
    forward(0)
    over_line(2)
    onward(0)
    weights = []
    for s in range(4):
        columns = [(hits[p] * routed[0][p : p + 1, :])[8 * s : 8 * s + 8] for p in range(8)]
        weight = jnp.concatenate(columns, axis=0).T
        weight = jnp.concatenate([weight[16 * i + 4 * s : 16 * i + 4 * s + 4] for i in range(4)])
        high = weight.astype(BF16)
        rest = weight - high.astype(F32)
        middle = rest.astype(BF16)
        low = (rest - middle.astype(F32)).astype(BF16)
        weights.append(jnp.concatenate([high, middle, low], axis=0))

    spread(3)
    forward(1)
    onward(1)
    spread(2)
    forward(3)
    onward(2)
    forward(2)

    def wait_weights(k):
        for copy in core_copies[k]:
            copy.wait_recv()

        @pl.when(core != odd)
        def _():
            for number in range(8):
                piece = wall.at[core, k, :, pl.ds(PART * number, PART)]
                pltpu.make_async_remote_copy(
                    src_ref=piece,
                    dst_ref=piece,
                    send_sem=wp_sem.at[0, k, number],
                    recv_sem=wp_sem.at[1, k, number],
                    device_id=across,
                    device_id_type=MESH,
                ).wait_recv()

    for copy in over_core:
        copy.wait_recv()
    wait_weights(0)
    wait_weights(1)

    into = wall.at[core, pl.ds(0, 2)]

    @pl.loop(0, 2)
    def _(h):
        taken = slots[pl.ds(1, 4), :, pl.ds(pl.multiple_of(16 * h, 16), 16), :]
        projected = matmul_nt(taken.reshape(256, WIDTH), into[...].reshape(256, WIDTH))
        projected = projected * (1.0 / math.sqrt(WIDTH))
        gate, up = projected[:, :128], projected[:, 128:]
        active[h] = (gate / (1.0 + jnp.exp(-gate)) * up).astype(BF16)

    wait_weights(2)
    keep(wall.at[odd], served_hbm)
    swaps = []
    for h in range(2):
        @pl.loop(0, 4)
        def _(i, h=h):
            span = pl.ds(pl.multiple_of(512 * i, 512), 512)
            out = matmul(active[h], wall[core, 2, :, span]) * (1.0 / math.sqrt(HIDDEN))
            out = out.reshape(4, 4, 16, 512)
            answers[2 * h, :, :, :, span] = out[:, :, 0:8].astype(BF16)
            answers[2 * h + 1, :, :, :, span] = out[:, :, 8:16].astype(BF16)

        for s in (2 * h, 2 * h + 1):
            for number in (3, 1):
                swaps.append(
                    send(
                        answers.at[s, number],
                        from_core.at[s, number // 2],
                        ret_sem,
                        (s, number // 2),
                        next_core,
                    )
                )

    over_y = []
    for s in range(4):
        swaps[2 * s].wait_recv()
        relay[s] = (answers[s, 2].astype(F32) + from_core[s, 1].astype(F32)).astype(BF16)
        over_y.append(send(relay.at[s], joined.at[s, 1], turn_sem, (s,), {Y_AXIS: other}))
    for s in range(4):
        swaps[2 * s + 1].wait_recv()
        joined[s, 0] = (answers[s, 0].astype(F32) + from_core[s, 0].astype(F32)).astype(BF16)

    over_x, over_z = {}, {}

    def along_x(s):
        over_y[s].wait_recv()
        over_x[s] = [
            send(joined.at[s, :, d], back.at[s, d], back_sem, (s, d), turn(X_AXIS, x, 4 - d))
            for d in (2, 1, 3)
        ]
        back[s, 0] = joined[s, :, 0]

    def to_rows(s):
        for copy in over_x[s]:
            copy.wait_recv()
        made = matmul(weights[s], back[s].reshape(64, WIDTH))
        made = made[0:16] + made[16:32] + made[32:48]
        for i in range(4):
            parts[s, i] = made[4 * i : 4 * i + 4].astype(BF16)
        over_z[s] = [
            send(
                parts.at[s, (zh + j) % 4],
                parts_in.at[s, j - 1],
                end_sem,
                (s, j - 1),
                turn(ZH_AXIS, zh, j),
            )
            for j in (2, 1, 3)
        ]

    along_x(0)
    along_x(1)
    to_rows(0)
    along_x(2)
    to_rows(1)
    along_x(3)
    to_rows(2)
    to_rows(3)
    for s in range(4):
        result = wide[pl.ds(4 * s, 4), :] + parts[s, zh].astype(F32)
        for copy in over_z[s]:
            copy.wait_recv()
        for j in range(3):
            result = result + parts_in[s, j].astype(F32)
        decoded_ref[s] = result.astype(BF16)
    keep(decoded_ref, decoded_hbm)
    for copy in stores:
        copy.wait()
    for copy in started:
        copy.wait_send()
    for copy, wanted in line_sends:

        @pl.when(wanted)
        def _(copy=copy):
            copy.wait_send()


def hand_out(*refs):
    sources, targets, held, in_sem, out_sem = refs[:5], refs[5:10], refs[10:15], refs[15], refs[16]
    pieces = [(i, ()) for i in (0, 1, 2)] + [(3, (k,)) for k in range(3)] + [(4, ())]

    def piece(refs, i, at):
        return refs[i].at[at] if at else refs[i]

    loads, stores = [], []
    for number, (i, at) in enumerate(pieces):
        loads.append(
            pltpu.make_async_copy(piece(sources, i, at), piece(held, i, at), in_sem.at[number])
        )
        loads[-1].start()
    for number, (i, at) in enumerate(pieces):
        loads[number].wait()
        stores.append(
            pltpu.make_async_copy(piece(held, i, at), piece(targets, i, at), out_sem.at[number])
        )
        stores[-1].start()
    for store in stores:
        store.wait()


def per_device(
    master, moment_one, moment_two, gradients, norm_gain, hidden_in, expert_ids, route_weights
):
    smem = pl.BlockSpec(memory_space=pltpu.SMEM)
    anywhere = pl.BlockSpec(memory_space=pltpu.HBM)
    flat = (384, PART)
    dma = pltpu.SemaphoreType.DMA
    out_shape = (
        jax.ShapeDtypeStruct(flat, F32),
        jax.ShapeDtypeStruct(flat, F32),
        jax.ShapeDtypeStruct(flat, F32),
        jax.ShapeDtypeStruct((3, 128, WIDTH), BF16),
        jax.ShapeDtypeStruct((4, 4, WIDTH), BF16),
    )
    results = pl.pallas_call(
        body,
        out_shape=out_shape,
        in_specs=[smem, smem] + [anywhere] * 6,
        out_specs=(anywhere,) * 5,
        scratch_shapes=[
            pltpu.VMEM(flat, F32),
            pltpu.VMEM(flat, F32),
            pltpu.VMEM(flat, F32),
            pltpu.VMEM((4, 4, WIDTH), BF16),
            pltpu.VMEM(flat, F32),
            pltpu.VMEM(flat, F32),
            pltpu.VMEM(flat, F32),
            pltpu.VMEM(flat, BF16),
            pltpu.VMEM((1, WIDTH), F32),
            pltpu.VMEM((4, 4, WIDTH), BF16),
            pltpu.VMEM((16, WIDTH), F32),
            pltpu.VMEM((4, 16, WIDTH), BF16),
            pltpu.VMEM((4, 4, 128), F32),
            pltpu.VMEM((4, 1, 128), F32),
            pltpu.VMEM((22, 1, 128), F32),
            pltpu.VMEM((3, 2, BLOCK, WIDTH), BF16),
            pltpu.VMEM((5, 4, BLOCK, WIDTH), BF16),
            pltpu.VMEM((4, 4, 4, 8, WIDTH), BF16),
            pltpu.VMEM((4, 2, 4, 8, WIDTH), BF16),
            pltpu.VMEM((4, 4, 8, WIDTH), BF16),
            pltpu.VMEM((4, 2, 4, 8, WIDTH), BF16),
            pltpu.VMEM((4, 4, 2, 8, WIDTH), BF16),
            pltpu.VMEM((4, 4, 4, WIDTH), BF16),
            pltpu.VMEM((4, 3, 4, WIDTH), BF16),
            pltpu.VMEM((3, 4, 32, PART), BF16),
            pltpu.VMEM((3, 4, 32, PART), BF16),
            pltpu.VMEM((3, 4, 32, PART), BF16),
            pltpu.VMEM((3, 4, 32, PART), BF16),
            pltpu.VMEM((3, 4, 32, PART), BF16),
            pltpu.VMEM((2, 3, 128, WIDTH), BF16),
            pltpu.VMEM((2, 256, 128), BF16),
            dma((6,)),
            dma((5,)),
            dma((2, 22)),
            dma((2, 3)),
            dma((2, 3)),
            dma((2, 3)),
            dma((2, 4)),
            dma((2, 2, 4)),
            dma((2, 4, 2)),
            dma((2, 4)),
            dma((2, 4, 4)),
            dma((2, 4, 3)),
            dma((2, 3, 3)),
            dma((2, 3, 3)),
            dma((2, 3, 3)),
            dma((2, 3, 4)),
            dma((2, 3, 4)),
            dma((2, 3, 8)),
        ],
        compiler_params=pltpu.CompilerParams(
            collective_id=0, has_side_effects=True, vmem_limit_bytes=56 * 1024 * 1024
        ),
        name="step",
    )(
        expert_ids.transpose(0, 2, 1),
        route_weights.transpose(0, 2, 1),
        master.reshape(flat),
        moment_one.reshape(flat),
        moment_two.reshape(flat),
        gradients.reshape(flat),
        norm_gain.reshape(1, WIDTH),
        hidden_in,
    )
    new_master, new_one, new_two, served, decoded = pl.pallas_call(
        hand_out,
        out_shape=out_shape,
        in_specs=[anywhere] * 5,
        out_specs=(anywhere,) * 5,
        scratch_shapes=[pltpu.VMEM(array.shape, array.dtype) for array in out_shape]
        + [dma((7,)), dma((7,))],
        name="hand_out",
    )(*results)
    return (
        new_master.reshape(master.shape),
        new_one.reshape(master.shape),
        new_two.reshape(master.shape),
        served,
        decoded,
    )


def solution(mesh):
    split = Mesh(mesh.devices.reshape(4, 4, 4, 4, 2), DP_TENSOR)
    sharded = P(None, None, DP, TENSOR)
    by_row = P(None, DP_TENSOR, None)
    return jax.shard_map(
        per_device,
        mesh=split,
        in_specs=(sharded, sharded, sharded, sharded, P(), by_row, by_row, by_row),
        out_specs=(sharded, sharded, sharded, P(None, DP, None), by_row),
        check_vma=False,
    )
```

```python
import math

import jax
import jax.numpy as jnp
from jax import lax
from jax.experimental import pallas as pl
from jax.experimental.pallas import tpu as pltpu
from jax.sharding import Mesh
from jax.sharding import PartitionSpec as P

DP = ("dp_0", "dp_1", "dp_2")
TENSOR = ("tensor_0", "tensor_1")
DP_TENSOR = DP + TENSOR
X_AXIS, Y_AXIS, ZH_AXIS, ZL_AXIS, C_AXIS = DP_TENSOR

MESH = pl.DeviceIdType.MESH
F32 = jnp.float32
BF16 = jnp.bfloat16

beta_one = 0.9
beta_two = 0.95
learn_rate = 0.02
decay_rate = 0.1
adam_eps = 1e-08
step_count = 10
norm_eps = 1e-06

WIDTH = 2048
PART = 256
HIDDEN = 1024
COUNT = 3 * 8 * 1024 * 2048
BLOCK = 32


def one_hot_rows(source_of):
    row = lax.broadcasted_iota(jnp.int32, (128, 128), 0)
    column = lax.broadcasted_iota(jnp.int32, (128, 128), 1)
    a, b, c, i = row // 32, (row // 8) % 4, (row // 2) % 4, row % 2
    return jnp.where(column == source_of(a, b, c, i), 1.0, 0.0).astype(BF16)


def matmul(left, right):
    return lax.dot_general(left, right, (((1,), (0,)), ((), ())), preferred_element_type=F32)


def matmul_nt(left, right):
    return lax.dot_general(left, right, (((1,), (1,)), ((), ())), preferred_element_type=F32)


def body(
    ids_ref,
    gates_ref,
    master_hbm,
    one_hbm,
    two_hbm,
    grad_hbm,
    gain_hbm,
    hidden_hbm,
    new_master_hbm,
    new_one_hbm,
    new_two_hbm,
    served_hbm,
    decoded_hbm,
    new_master_ref,
    new_one_ref,
    new_two_ref,
    decoded_ref,
    master_ref,
    one_ref,
    two_ref,
    grad_ref,
    gain_ref,
    hidden_ref,
    wide,
    zrows,
    meta,
    sums_out,
    sums_in,
    stage,
    slots,
    answers,
    from_core,
    relay,
    joined,
    back,
    parts,
    parts_in,
    wz_out,
    wz_in,
    wy_out,
    wy_in,
    wx_out,
    wall,
    active,
    in_sem,
    out_sem,
    sum_sem,
    meta_sem,
    tok_sem,
    x_sem,
    y_sem,
    core_sem,
    ret_sem,
    turn_sem,
    back_sem,
    end_sem,
    wz_sem,
    wy_sem,
    wx_sem,
    wl_sem,
    wc_sem,
    wp_sem,
):
    x = lax.axis_index(X_AXIS)
    y = lax.axis_index(Y_AXIS)
    zh = lax.axis_index(ZH_AXIS)
    zl = lax.axis_index(ZL_AXIS)
    core = lax.axis_index(C_AXIS)
    pair = y // 2
    odd = y % 2
    partner = y + 1 - 2 * odd
    other = (y + 3 + 2 * odd) % 4
    next_core = {C_AXIS: 1 - core}
    started = []

    def send(source, target, sems, index, device):
        copy = pltpu.make_async_remote_copy(
            src_ref=source,
            dst_ref=target,
            send_sem=sems.at[(0,) + index],
            recv_sem=sems.at[(1,) + index],
            device_id=device,
            device_id_type=MESH,
        )
        copy.start()
        started.append(copy)
        return copy

    def turn(axis, me, j):
        return {axis: (me + j) % 4}

    def along_z(j):
        z = (4 * zh + zl + j) % 16
        return {ZH_AXIS: z // 4, ZL_AXIS: z % 4}

    barrier = pltpu.get_barrier_semaphore()
    peers = [along_z(j) for j in (8, 7, 9, 6, 10, 5, 11, 4, 12, 3, 13, 2, 14, 1, 15)]
    plane = [
        {X_AXIS: (x + i) % 4, Y_AXIS: (y + j) % 4}
        for i in (2, 1, 3, 0)
        for j in (2, 1, 3, 0)
        if i or j
    ]
    peers += plane
    peers += [{Y_AXIS: partner, C_AXIS: 1 - core}, next_core]
    for peer in peers:
        pl.semaphore_signal(barrier, inc=1, device_id=peer, device_id_type=MESH)
    loads = [
        pltpu.make_async_copy(source, target, in_sem.at[number])
        for number, (source, target) in enumerate(
            (
                (hidden_hbm, hidden_ref),
                (gain_hbm, gain_ref),
                (grad_hbm, grad_ref),
                (master_hbm, master_ref),
                (one_hbm, one_ref),
                (two_hbm, two_ref),
            )
        )
    ]
    for load in loads:
        load.start()

    meta_row = lax.broadcasted_iota(jnp.int32, (8, 128), 0)
    meta_lane = lax.broadcasted_iota(jnp.int32, (8, 128), 1) - zh * 16
    tile = jnp.zeros((8, 128), F32)
    for s in range(4):
        for r in range(4):
            spot = meta_lane == 4 * s + r
            for k in range(2):
                tile = jnp.where(spot & (meta_row == k), ids_ref[s, k, r].astype(F32), tile)
                tile = jnp.where(spot & (meta_row == 2 + k), gates_ref[s, k, r], tile)
    meta[0] = tile[0:4]
    loads[0].wait()
    loads[1].wait()
    for s in range(4):
        wide[pl.ds(4 * s, 4), :] = hidden_ref[s].astype(F32)
    rows = wide[...]
    factor = lax.rsqrt(jnp.mean(rows * rows, axis=1, keepdims=True) + norm_eps)
    normed = rows * factor * gain_ref[...]
    zrows[zh] = normed.astype(BF16)
    loads[2].wait()

    def add_block(block, squares):
        values = grad_ref[pl.ds(pl.multiple_of(32 * block, 32), 32), :].astype(F32)
        values = values * values
        for i in range(4):
            for h in range(2):
                squares = squares + values[8 * i : 8 * i + 8, 128 * h : 128 * h + 128]
        return squares

    squares = lax.fori_loop(0, 12, add_block, jnp.zeros((8, 128), F32))
    squares = jnp.sum(squares, axis=0, keepdims=True)
    sums_out[0] = squares
    pl.semaphore_wait(barrier, len(peers))

    slot = 0
    token_copies = []
    for phase, devices in enumerate(
        (
            [along_z(j) for j in (8, 7, 9, 6, 10, 5, 11, 4, 12, 3, 13, 2, 14, 1, 15)],
            plane,
            [next_core],
        )
    ):
        copies = [
            send(sums_out.at[phase], sums_in.at[slot + i], sum_sem, (slot + i,), device)
            for i, device in enumerate(devices)
        ]
        if phase == 0:
            for j in (2, 1, 3):
                token_copies.append(
                    send(meta.at[0], meta.at[j], meta_sem, (j - 1,), turn(ZH_AXIS, zh, j))
                )
                token_copies.append(
                    send(zrows.at[zh], zrows.at[zh], tok_sem, (j - 1,), turn(ZH_AXIS, zh, j))
                )
        if phase == 2:
            permute_z = one_hot_rows(lambda a, b, c, i: ((b * 4 + c) * 4 + a) * 2 + i)
            permute_y = one_hot_rows(lambda a, b, c, i: ((c * 4 + b) * 4 + a) * 2 + i)
            permute_x = one_hot_rows(lambda a, b, c, i: ((b * 4 + a) * 4 + c) * 2 + i)
            for load in loads[3:]:
                load.wait()
        for i, copy in enumerate(copies):
            copy.wait_recv()
            squares = squares + sums_in[slot + i]
        slot += len(copies)
        if phase < 2:
            sums_out[phase + 1] = squares
    total = jnp.sum(squares, axis=(0, 1), keepdims=True)
    clip = jnp.minimum(1.0, lax.rsqrt(total * (1.0 / COUNT) + norm_eps))

    x_copies = {}
    hits = []
    routed = []

    def pick():
        for copy in token_copies:
            copy.wait_recv()
        routes = meta[0] + meta[1] + meta[2] + meta[3]
        id_one, id_two = routes[0:1, 0:64], routes[1:2, 0:64]
        gate_one, gate_two = routes[2:3, 0:64], routes[3:4, 0:64]
        gate_sum = gate_one + gate_two
        share_one, share_two = gate_one / gate_sum, gate_two / gate_sum
        place = lax.broadcasted_iota(jnp.int32, (8, 64), 0)
        expert = (2 * ((x + place // 2) % 4) + (pair + place % 2) % 2).astype(F32)
        names_one = jnp.where(id_one == expert, 1.0, 0.0)
        names_two = jnp.where(id_two == expert, 1.0, 0.0)
        named = names_one + names_two
        share = names_one * share_one + names_two * share_two
        above = lax.broadcasted_iota(jnp.int32, (64, 64), 0)
        below = lax.broadcasted_iota(jnp.int32, (64, 64), 1)
        before = jnp.where((above // 4 == below // 4) & (above < below), 1.0, 0.0).astype(BF16)
        earlier = matmul(named.astype(BF16), before)
        slot_row = lax.broadcasted_iota(jnp.int32, (32, 64), 0)
        row_lane = lax.broadcasted_iota(jnp.int32, (32, 64), 1)
        same_block = jnp.where(
            (slot_row // 8 == (row_lane // 4) % 4) & ((slot_row // 2) % 4 == row_lane // 16), 1.0, 0.0
        )
        slot_number = (slot_row % 2).astype(F32)
        hits[:] = [jnp.where(earlier[p : p + 1, :] == slot_number, same_block, 0.0) for p in range(8)]
        token_rows = zrows[...].reshape(64, WIDTH)
        for d in (0, 2, 1, 3):
            picks = [hits[2 * d + r] * named[2 * d + r : 2 * d + r + 1, :] for r in (1, 0)]
            chosen = matmul(jnp.concatenate(picks, axis=0).astype(BF16), token_rows)
            chosen = chosen.astype(BF16).reshape(2, BLOCK, WIDTH)
            if d == 0:
                slots[0, 0] = chosen[0]
                slots[1, 0] = chosen[1]
            else:
                stage[d - 1] = chosen
                x_copies[d] = send(
                    stage.at[d - 1], slots.at[pl.ds(0, 2), d], x_sem, (d - 1,), turn(X_AXIS, x, d)
                )
        routed.append(share)

    first_fix = 1.0 / (1.0 - beta_one**step_count)
    second_fix = 1.0 / (1.0 - beta_two**step_count)
    z_copies = []
    stores = []

    def keep(source, target):
        copy = pltpu.make_async_copy(source, target, out_sem.at[len(stores)])
        copy.start()
        stores.append(copy)

    for k in range(3):
        @pl.loop(0, 4)
        def _(block, k=k):
            at = pl.ds(pl.multiple_of(128 * k + 32 * block, 32), 32)
            scaled = grad_ref[at, :].astype(F32) * clip
            first = beta_one * one_ref[at, :] + (1.0 - beta_one) * scaled
            second = beta_two * two_ref[at, :] + (1.0 - beta_two) * scaled * scaled
            update = first * first_fix / (jnp.sqrt(second * second_fix) + adam_eps)
            old = master_ref[at, :]
            new_master_ref[at, :] = old - learn_rate * (update + decay_rate * old)
            new_one_ref[at, :] = first
            new_two_ref[at, :] = second

        rounded = new_master_ref[pl.ds(128 * k, 128), :].astype(BF16)
        wz_out[k] = matmul(permute_z, rounded).astype(BF16).reshape(4, 32, PART)
        for j in (2, 1, 3):
            z_copies.append(
                send(
                    wz_out.at[k, (zh + j) % 4],
                    wz_in.at[k, zh],
                    wz_sem,
                    (k, j - 1),
                    turn(ZH_AXIS, zh, j),
                )
            )
        wz_in[k, zh] = wz_out[k, zh]
        if k == 0:
            pick()
    keep(new_master_ref, new_master_hbm)
    keep(new_one_ref, new_one_hbm)
    keep(new_two_ref, new_two_hbm)

    over_y, over_core = {}, []

    def spread(d):
        if d:
            x_copies[d].wait_recv()
        over_y[d] = send(slots.at[0, d], slots.at[3, d], y_sem, (d,), {Y_AXIS: other})
        over_core.append(send(slots.at[1, d], slots.at[2, d], core_sem, (0, d), next_core))

    def forward(d):
        over_y[d].wait_recv()
        over_core.append(send(slots.at[3, d], slots.at[4, d], core_sem, (1, d), next_core))

    def columns_of(position):
        return pl.ds(pl.multiple_of((2 * position + core) * PART, PART), PART)

    own_rows = pl.ds(pl.multiple_of(32 * x, 32), 32)
    across = {Y_AXIS: partner, C_AXIS: odd}
    y_copies, wx_copies, core_copies, line_sends = {}, {}, {0: [], 1: [], 2: []}, []

    def over_wy(k):
        for copy in z_copies[3 * k : 3 * k + 3]:
            copy.wait_recv()
        gathered = wz_in[k].reshape(128, PART)
        wy_out[k] = matmul(permute_y, gathered).astype(BF16).reshape(4, 32, PART)
        y_copies[k] = [
            send(wy_out.at[k, (y + j) % 4], wy_in.at[k, y], wy_sem, (k, j - 1), turn(Y_AXIS, y, j))
            for j in (2, 1, 3)
        ]
        wy_in[k, y] = wy_out[k, y]

    def over_wx(k):
        for copy in y_copies[k]:
            copy.wait_recv()
        gathered = wy_in[k].reshape(128, PART)
        wx_out[k] = matmul(permute_x, gathered).astype(BF16).reshape(4, 32, PART)
        wx_copies[k] = [
            send(
                wx_out.at[k, (x + j) % 4],
                wall.at[odd, k, own_rows, columns_of(zl)],
                wx_sem,
                (k, j - 1),
                turn(X_AXIS, x, j),
            )
            for j in (2, 1, 3)
        ]
        wall[odd, k, own_rows, columns_of(zl)] = wx_out[k, x]

    def line_copy(k, position, number, arrival, target):
        piece = wall.at[odd, k, :, columns_of(position)]
        return pltpu.make_async_remote_copy(
            src_ref=piece,
            dst_ref=piece,
            send_sem=wl_sem.at[0, k, number],
            recv_sem=wl_sem.at[1, k, arrival],
            device_id={ZL_AXIS: target},
            device_id_type=MESH,
        )

    def line_send(copy, wanted):
        @pl.when(wanted)
        def _():
            copy.start()

        line_sends.append((copy, wanted))

    def share_out(k, j, position):
        piece = wall.at[odd, k, :, columns_of(position)]
        send(piece, piece, wp_sem, (k, 2 * j + core), across)
        core_copies[k].append(send(piece, piece, wc_sem, (k, j), next_core))

    def over_line(k):
        for copy in wx_copies[k]:
            copy.wait_recv()
        for j in (2, 1, 3):
            near = True if j == 2 else (zl != (3 if j == 1 else 0))
            line_send(line_copy(k, zl, j - 1, j - 1, (zl + j) % 4), near)
        share_out(k, 0, zl)

    late = jnp.where(zl == 0, 1, 3)
    relay_to = jnp.where(zl == 2, 3, 0)

    def onward(k):
        for j in (2, 4 - late, late):
            position = (zl + 4 - j) % 4
            line_copy(k, position, j - 1, j - 1, zl).wait_recv()
            if isinstance(j, int):
                relayed = line_copy(k, position, 3, jnp.where(zl == 2, 2, 0), relay_to)
                line_send(relayed, (zl == 1) | (zl == 2))
            share_out(k, j, position)

    over_wy(0)
    over_wy(1)
    over_wx(0)
    over_wy(2)
    over_wx(1)
    over_line(0)
    spread(0)
    over_wx(2)
    over_line(1)
    spread(1)
    forward(0)
    over_line(2)
    onward(0)
    weights = []
    for s in range(4):
        columns = [(hits[p] * routed[0][p : p + 1, :])[8 * s : 8 * s + 8] for p in range(8)]
        weight = jnp.concatenate(columns, axis=0).T
        weight = jnp.concatenate([weight[16 * i + 4 * s : 16 * i + 4 * s + 4] for i in range(4)])
        high = weight.astype(BF16)
        rest = weight - high.astype(F32)
        middle = rest.astype(BF16)
        low = (rest - middle.astype(F32)).astype(BF16)
        weights.append(jnp.concatenate([high, middle, low], axis=0))

    spread(3)
    forward(1)
    onward(1)
    spread(2)
    forward(3)
    onward(2)
    forward(2)

    def wait_weights(k):
        for copy in core_copies[k]:
            copy.wait_recv()

        @pl.when(core != odd)
        def _():
            for number in range(8):
                piece = wall.at[core, k, :, pl.ds(PART * number, PART)]
                pltpu.make_async_remote_copy(
                    src_ref=piece,
                    dst_ref=piece,
                    send_sem=wp_sem.at[0, k, number],
                    recv_sem=wp_sem.at[1, k, number],
                    device_id=across,
                    device_id_type=MESH,
                ).wait_recv()

    for copy in over_core:
        copy.wait_recv()
    wait_weights(0)
    wait_weights(1)

    into = wall.at[core, pl.ds(0, 2)]

    @pl.loop(0, 2)
    def _(h):
        taken = slots[pl.ds(1, 4), :, pl.ds(pl.multiple_of(16 * h, 16), 16), :]
        projected = matmul_nt(taken.reshape(256, WIDTH), into[...].reshape(256, WIDTH))
        projected = projected * (1.0 / math.sqrt(WIDTH))
        gate, up = projected[:, :128], projected[:, 128:]
        active[h] = (gate / (1.0 + jnp.exp(-gate)) * up).astype(BF16)

    wait_weights(2)
    keep(wall.at[odd], served_hbm)
    swaps = []
    for h in range(2):
        @pl.loop(0, 4)
        def _(i, h=h):
            span = pl.ds(pl.multiple_of(512 * i, 512), 512)
            out = matmul(active[h], wall[core, 2, :, span]) * (1.0 / math.sqrt(HIDDEN))
            out = out.reshape(4, 4, 16, 512)
            answers[2 * h, :, :, :, span] = out[:, :, 0:8].astype(BF16)
            answers[2 * h + 1, :, :, :, span] = out[:, :, 8:16].astype(BF16)

        for s in (2 * h, 2 * h + 1):
            for number in (3, 1):
                swaps.append(
                    send(
                        answers.at[s, number],
                        from_core.at[s, number // 2],
                        ret_sem,
                        (s, number // 2),
                        next_core,
                    )
                )

    over_y = []
    for s in range(4):
        swaps[2 * s].wait_recv()
        relay[s] = (answers[s, 2].astype(F32) + from_core[s, 1].astype(F32)).astype(BF16)
        over_y.append(send(relay.at[s], joined.at[s, 1], turn_sem, (s,), {Y_AXIS: other}))
    for s in range(4):
        swaps[2 * s + 1].wait_recv()
        joined[s, 0] = (answers[s, 0].astype(F32) + from_core[s, 0].astype(F32)).astype(BF16)

    over_x, over_z = {}, {}

    def along_x(s):
        over_y[s].wait_recv()
        over_x[s] = [
            send(joined.at[s, :, d], back.at[s, d], back_sem, (s, d), turn(X_AXIS, x, 4 - d))
            for d in (2, 1, 3)
        ]
        back[s, 0] = joined[s, :, 0]

    def to_rows(s):
        for copy in over_x[s]:
            copy.wait_recv()
        made = matmul(weights[s], back[s].reshape(64, WIDTH))
        made = made[0:16] + made[16:32] + made[32:48]
        for i in range(4):
            parts[s, i] = made[4 * i : 4 * i + 4].astype(BF16)
        over_z[s] = [
            send(
                parts.at[s, (zh + j) % 4],
                parts_in.at[s, j - 1],
                end_sem,
                (s, j - 1),
                turn(ZH_AXIS, zh, j),
            )
            for j in (2, 1, 3)
        ]

    along_x(0)
    along_x(1)
    to_rows(0)
    along_x(2)
    to_rows(1)
    along_x(3)
    to_rows(2)
    to_rows(3)
    for s in range(4):
        result = wide[pl.ds(4 * s, 4), :] + parts[s, zh].astype(F32)
        for copy in over_z[s]:
            copy.wait_recv()
        for j in range(3):
            result = result + parts_in[s, j].astype(F32)
        decoded_ref[s] = result.astype(BF16)
    keep(decoded_ref, decoded_hbm)
    for copy in stores:
        copy.wait()
    for copy in started:
        copy.wait_send()
    for copy, wanted in line_sends:

        @pl.when(wanted)
        def _(copy=copy):
            copy.wait_send()


def hand_out(*refs):
    sources, targets, held, in_sem, out_sem = refs[:5], refs[5:10], refs[10:15], refs[15], refs[16]
    pieces = [(i, ()) for i in (0, 1, 2)] + [(3, (k,)) for k in range(3)] + [(4, ())]

    def piece(refs, i, at):
        return refs[i].at[at] if at else refs[i]

    loads, stores = [], []
    for number, (i, at) in enumerate(pieces):
        loads.append(
            pltpu.make_async_copy(piece(sources, i, at), piece(held, i, at), in_sem.at[number])
        )
        loads[-1].start()
    for number, (i, at) in enumerate(pieces):
        loads[number].wait()
        stores.append(
            pltpu.make_async_copy(piece(held, i, at), piece(targets, i, at), out_sem.at[number])
        )
        stores[-1].start()
    for store in stores:
        store.wait()


def per_device(
    master, moment_one, moment_two, gradients, norm_gain, hidden_in, expert_ids, route_weights
):
    smem = pl.BlockSpec(memory_space=pltpu.SMEM)
    anywhere = pl.BlockSpec(memory_space=pltpu.HBM)
    flat = (384, PART)
    dma = pltpu.SemaphoreType.DMA
    out_shape = (
        jax.ShapeDtypeStruct(flat, F32),
        jax.ShapeDtypeStruct(flat, F32),
        jax.ShapeDtypeStruct(flat, F32),
        jax.ShapeDtypeStruct((3, 128, WIDTH), BF16),
        jax.ShapeDtypeStruct((4, 4, WIDTH), BF16),
    )
    results = pl.pallas_call(
        body,
        out_shape=out_shape,
        in_specs=[smem, smem] + [anywhere] * 6,
        out_specs=(anywhere,) * 5,
        scratch_shapes=[
            pltpu.VMEM(flat, F32),
            pltpu.VMEM(flat, F32),
            pltpu.VMEM(flat, F32),
            pltpu.VMEM((4, 4, WIDTH), BF16),
            pltpu.VMEM(flat, F32),
            pltpu.VMEM(flat, F32),
            pltpu.VMEM(flat, F32),
            pltpu.VMEM(flat, BF16),
            pltpu.VMEM((1, WIDTH), F32),
            pltpu.VMEM((4, 4, WIDTH), BF16),
            pltpu.VMEM((16, WIDTH), F32),
            pltpu.VMEM((4, 16, WIDTH), BF16),
            pltpu.VMEM((4, 4, 128), F32),
            pltpu.VMEM((3, 1, 128), F32),
            pltpu.VMEM((31, 1, 128), F32),
            pltpu.VMEM((3, 2, BLOCK, WIDTH), BF16),
            pltpu.VMEM((5, 4, BLOCK, WIDTH), BF16),
            pltpu.VMEM((4, 4, 4, 8, WIDTH), BF16),
            pltpu.VMEM((4, 2, 4, 8, WIDTH), BF16),
            pltpu.VMEM((4, 4, 8, WIDTH), BF16),
            pltpu.VMEM((4, 2, 4, 8, WIDTH), BF16),
            pltpu.VMEM((4, 4, 2, 8, WIDTH), BF16),
            pltpu.VMEM((4, 4, 4, WIDTH), BF16),
            pltpu.VMEM((4, 3, 4, WIDTH), BF16),
            pltpu.VMEM((3, 4, 32, PART), BF16),
            pltpu.VMEM((3, 4, 32, PART), BF16),
            pltpu.VMEM((3, 4, 32, PART), BF16),
            pltpu.VMEM((3, 4, 32, PART), BF16),
            pltpu.VMEM((3, 4, 32, PART), BF16),
            pltpu.VMEM((2, 3, 128, WIDTH), BF16),
            pltpu.VMEM((2, 256, 128), BF16),
            dma((6,)),
            dma((5,)),
            dma((2, 31)),
            dma((2, 3)),
            dma((2, 3)),
            dma((2, 3)),
            dma((2, 4)),
            dma((2, 2, 4)),
            dma((2, 4, 2)),
            dma((2, 4)),
            dma((2, 4, 4)),
            dma((2, 4, 3)),
            dma((2, 3, 3)),
            dma((2, 3, 3)),
            dma((2, 3, 3)),
            dma((2, 3, 4)),
            dma((2, 3, 4)),
            dma((2, 3, 8)),
        ],
        compiler_params=pltpu.CompilerParams(
            collective_id=0, has_side_effects=True, vmem_limit_bytes=56 * 1024 * 1024
        ),
        name="step",
    )(
        expert_ids.transpose(0, 2, 1),
        route_weights.transpose(0, 2, 1),
        master.reshape(flat),
        moment_one.reshape(flat),
        moment_two.reshape(flat),
        gradients.reshape(flat),
        norm_gain.reshape(1, WIDTH),
        hidden_in,
    )
    new_master, new_one, new_two, served, decoded = pl.pallas_call(
        hand_out,
        out_shape=out_shape,
        in_specs=[anywhere] * 5,
        out_specs=(anywhere,) * 5,
        scratch_shapes=[pltpu.VMEM(array.shape, array.dtype) for array in out_shape]
        + [dma((7,)), dma((7,))],
        name="hand_out",
    )(*results)
    return (
        new_master.reshape(master.shape),
        new_one.reshape(master.shape),
        new_two.reshape(master.shape),
        served,
        decoded,
    )


def solution(mesh):
    split = Mesh(mesh.devices.reshape(4, 4, 4, 4, 2), DP_TENSOR)
    sharded = P(None, None, DP, TENSOR)
    by_row = P(None, DP_TENSOR, None)
    return jax.shard_map(
        per_device,
        mesh=split,
        in_specs=(sharded, sharded, sharded, sharded, P(), by_row, by_row, by_row),
        out_specs=(sharded, sharded, sharded, P(None, DP, None), by_row),
        check_vma=False,
    )
```
